256 devices in a mesh: sp: 64 (over x, z, core), bd: 4 (over y).
Axes of the slice: x: 4, y: 4, z: 8, core: 2. Of those that a mesh axis runs over, the one named last changes fastest.
Arguments:
- cube: float32 [4, 768, 32, 2048], P('bd', 'sp'), may hold values from 0.02 to 25
- taps_x: float32 [4, 768, 25], P('bd', 'sp'), may hold values from 0.1 to 1
- taps_y: float32 [4, 768, 25], P('bd', 'sp'), may hold values from 0.1 to 1
- factor_w: float32 [4, 768, 48], P('bd'), may hold values from 0.1 to 1
- factor_h: float32 [48, 32, 2048], P(None, None, 'sp'), may hold values from 0.1 to 1
Outputs:
- w_next: float32 [4, 768, 48], P('bd')
- h_next: float32 [48, 32, 2048], P(None, None, 'sp')
The draws below stay inside these ranges and needn't reach their ends.
All inputs are finite; a program needn't handle non-finite values.
Results may differ from the reference program's by a relative error of at most 0.000071.
Values sent between devices are 32-bit elements; how exact they have to be, the bound alone decides.
A program may use at most 128 MiB of HBM per device.

```python
import math
import jax
import jax.numpy as jnp
from jax import lax

SY = 32
R = 48
TAPS = 25
BANDS = 4
LB = 768
SX = 2048


def draw_cube(key, part):
    cube_shape = (BANDS, LB, SY, SX)
    along_strip = jnp.arange(SX, dtype=jnp.float32).reshape(1, 1, 1, SX)
    across_strip = jnp.arange(SY, dtype=jnp.float32).reshape(1, 1, SY, 1)
    continuum_key = jax.random.fold_in(key, 1)
    noise_key = jax.random.fold_in(key, 2)
    continuum = jnp.exp(jax.random.uniform(continuum_key, (BANDS, LB, 1, 1), jnp.float32, math.log(0.2), 0.0))
    summed_flux = continuum
    for source in range(4):
        source_key = jax.random.fold_in(key, 10 + source)
        spectrum_key, scale_key, phase_key = jax.random.split(source_key, 3)
        spectrum = jnp.exp(jax.random.uniform(spectrum_key, (BANDS, LB, 1, 1), jnp.float32, -1.0, 1.0))
        spatial_scales = jnp.exp(jax.random.uniform(scale_key, (3,), jnp.float32, math.log(30.0), math.log(300.0)))
        phases = jax.random.uniform(phase_key, (3,), jnp.float32, 0.0, 2.0 * math.pi)
        profile = jnp.cos(2.0 * math.pi * along_strip / spatial_scales[0] + phases[0])
        profile = profile + jnp.cos(2.0 * math.pi * along_strip / spatial_scales[1] + phases[1])
        profile = profile + jnp.cos(2.0 * math.pi * across_strip / spatial_scales[2] + phases[2])
        summed_flux = summed_flux + spectrum * jnp.exp(0.5 * profile)
    voxel_factor = jnp.exp(jax.random.uniform(noise_key, cube_shape, jnp.float32, math.log(0.5), math.log(2.0)))
    return (0.25 * summed_flux * voxel_factor).astype(jnp.float32)


def steps_of(key, dims, shards, smallest, top_value):
    def one(position, blocks):
        heights = jax.random.uniform(jax.random.fold_in(jax.random.fold_in(key, 6), position), (blocks,), jnp.float32, smallest / len(shards), top_value / len(shards))
        return jnp.repeat(jnp.exp(heights), dims[position] // blocks).reshape((-1,) + (1,) * (len(dims) - position - 1))

    level = one(*shards[0])
    for cut in shards[1:]:
        level = level * one(*cut)
    return level


def setup_inputs(seed: int = 0) -> dict:
    arg_keys = jax.random.split(jax.random.key(seed), 6)
    return {
        "cube": draw_cube(jax.random.fold_in(arg_keys[5], 71), 0),
        "taps_x": jnp.clip(jnp.exp(math.log(1.0) - 2.3025851 * jax.random.uniform(arg_keys[1], (BANDS, LB, TAPS), jnp.float32) ** steps_of(arg_keys[1], (BANDS, LB, TAPS), ((0, 4), (1, 64)), -0.2, 0.2)), 0.1, 1.0),
        "taps_y": jnp.clip(jnp.exp(math.log(1.0) - 2.3025851 * jax.random.uniform(arg_keys[2], (BANDS, LB, TAPS), jnp.float32) ** steps_of(arg_keys[2], (BANDS, LB, TAPS), ((0, 4), (1, 64)), -0.2, 0.2)), 0.1, 1.0),
        "factor_w": jnp.clip(jnp.exp(math.log(1.0) - 2.3025851 * jax.random.uniform(arg_keys[3], (BANDS, LB, R), jnp.float32) ** steps_of(arg_keys[3], (BANDS, LB, R), ((0, 4),), -0.2, 0.2)), 0.1, 1.0),
        "factor_h": jnp.clip(jnp.exp(math.log(1.0) - 2.3025851 * jax.random.uniform(arg_keys[4], (R, SY, SX), jnp.float32) ** steps_of(arg_keys[4], (R, SY, SX), ((2, 64),), -0.2, 0.2)), 0.1, 1.0),
    }


def normalized(kernel):
    return kernel / jnp.sum(kernel, axis=-1, keepdims=True)


def blur_plane(items):
    image_plane, kernel_x, kernel_y = items
    margin = (kernel_x.shape[0] - 1) // 2
    height = image_plane.shape[0]
    length = image_plane.shape[1]
    padded = jnp.pad(image_plane, ((margin, margin), (0, 0)))
    summed = jnp.zeros_like(image_plane)
    for index in range(kernel_y.shape[0]):
        summed = summed + kernel_y[index] * padded[index:index + height, :]
    padded = jnp.pad(summed, ((0, 0), (margin, margin)))
    result = jnp.zeros_like(image_plane)
    for index in range(kernel_x.shape[0]):
        result = result + kernel_x[index] * padded[:, index:index + length]
    return result


def reference(cube, taps_x, taps_y, factor_w, factor_h):
    highest = lax.Precision.HIGHEST
    bands, planes, height, length = cube.shape
    rank = factor_w.shape[2]
    kernel_x = normalized(taps_x).reshape(bands * planes, -1)
    kernel_y = normalized(taps_y).reshape(bands * planes, -1)
    flat_cube = cube.reshape(bands * planes, height, length)
    blurred = lax.map(blur_plane, (flat_cube, kernel_x, kernel_y))
    matrix_x = blurred.reshape(bands * planes, height * length)
    matrix_w = factor_w.reshape(bands * planes, rank)
    matrix_h = factor_h.reshape(rank, height * length)
    numer_h = jnp.dot(matrix_w.T, matrix_x, precision=highest)
    gram_w = jnp.dot(matrix_w.T, matrix_w, precision=highest)
    h_next = matrix_h * numer_h / jnp.dot(gram_w, matrix_h, precision=highest)
    numer_w = jnp.dot(matrix_x, h_next.T, precision=highest)
    gram_h = jnp.dot(h_next, h_next.T, precision=highest)
    w_next = matrix_w * numer_w / jnp.dot(matrix_w, gram_h, precision=highest)
    return w_next.reshape(bands, planes, rank), h_next.reshape(rank, height, length)
```

```python
import functools

import jax
import jax.numpy as jnp
from jax import lax
from jax.experimental import pallas as pl
from jax.experimental.pallas import tpu as pltpu
from jax.sharding import PartitionSpec as P

HI = lax.Precision.HIGHEST
MESH = pl.DeviceIdType.MESH
NC = 2
F32 = jnp.float32


def normalized(kernel):
    return kernel / jnp.sum(kernel, axis=-1, keepdims=True)


def row_table(kernel_y, size):
    taps = kernel_y.shape[-1]
    margin = (taps - 1) // 2
    shape = (size, size, taps)
    out_i, in_i, tap = (lax.broadcasted_iota(jnp.int32, shape, d) for d in range(3))
    select = (tap == in_i - out_i + margin).astype(F32)
    return jnp.einsum("pk,oik->poi", kernel_y, select, precision=HI)


def column_table(kernel_x):
    taps = kernel_x.shape[-1]
    margin = (taps - 1) // 2
    shape = (256, 128, taps)
    in_i, out_i, tap = (lax.broadcasted_iota(jnp.int32, shape, d) for d in range(3))
    centre = (in_i < 128) & (tap == in_i - out_i + margin)
    edge = in_i - 128
    left = (in_i >= 128) & (tap == edge - 128 - out_i + margin)
    right = (in_i >= 128) & (tap == edge + 128 - out_i + margin)
    select = (centre | left | right).astype(F32)
    return jnp.einsum("pk,iok->pio", kernel_x, select, precision=HI)


def dot(a, b):
    return lax.dot_general(a, b, (((1,), (0,)), ((), ())), precision=HI, preferred_element_type=F32)


def dot_t(a, b):
    return lax.dot_general(a, b, (((1,), (1,)), ((), ())), precision=HI, preferred_element_type=F32)


def pad_lanes(a):
    return jnp.concatenate([a, jnp.zeros((a.shape[0], 128 - a.shape[1]), F32)], axis=1)


def kernel(geo, cube, table_x, table_y, w_t, h_in, w_out, h_out,
           send, recv, wm_send, wm_recv, rs_send, rs_recv, hz_send, hz_recv, hy_recv,
           wy_send, wy_recv, wx_send, wx_recv, wz_send, wz_recv,
           a_ss, a_rs, m_ss, m_rs, z_ss, z_rs, g_ss, g_rs, y_ss, y_rs,
           wy_ss, wy_rs, wx_ss, wx_rs, wz_ss, wz_rs):
    nx, ny, nz, planes, chunk = geo
    nh = nz // 4
    rpp = nh * 8
    nxc = nx * NC
    nu = ny * nxc
    pb = nxc * planes
    ptot = ny * pb
    zs = NC * planes
    rank = w_t.shape[0]
    sp = lax.axis_index("sp")
    y = lax.axis_index("bd")
    c = lax.rem(sp, NC)
    z = lax.rem(sp // NC, nz)
    x = sp // (NC * nz)
    xc = x * NC + c
    u = y * nxc + xc

    def dev_u(t):
        tx = lax.rem(t, nxc)
        return (((tx // NC) * nz + z) * NC + lax.rem(tx, NC), t // nxc)

    def dev_z(t):
        return ((x * nz + t) * NC + c, y)

    def dev_y(t):
        return (sp, t)

    def dev_xc(t):
        return (((t // NC) * nz + z) * NC + lax.rem(t, NC), y)

    barrier = pltpu.get_barrier_semaphore()

    @pl.loop(1, nu)
    def _(k):
        pl.semaphore_signal(barrier, inc=1, device_id=dev_u(lax.rem(u + k, nu)), device_id_type=MESH)

    @pl.loop(1, nz)
    def _(k):
        pl.semaphore_signal(barrier, inc=1, device_id=dev_z(lax.rem(z + k, nz)), device_id_type=MESH)

    def peers(n, me, dev, src, dst, ss, rs):
        def make(k):
            t = lax.rem(me + k, n)
            return pltpu.make_async_remote_copy(src_ref=src(t), dst_ref=dst, send_sem=ss.at[k], recv_sem=rs.at[k],
                                                device_id=dev(t), device_id_type=MESH)
        return make

    def start(n, make):
        @pl.loop(1, n)
        def _(k):
            make(k).start()

    def wait_recv(n, make):
        @pl.loop(1, n)
        def _(k):
            make(k).wait_recv()

    def wait_send(n, make):
        @pl.loop(1, n)
        def _(k):
            make(k).wait_send()

    l_i = lax.broadcasted_iota(jnp.int32, (w_t.shape[1], 128), 0)
    j_i = lax.broadcasted_iota(jnp.int32, (w_t.shape[1], 128), 1)
    xj = jnp.zeros_like(j_i)
    for i in range(1, nx):
        xj = xj + jnp.where(j_i >= zs * i, 1, 0)
    target = xj * (nz * zs) + z * zs + (j_i - zs * xj)
    pick = jnp.where((l_i == target) & (j_i < pb), 1.0, 0.0).astype(F32)
    w_all = w_t[...]
    w_slice = dot(w_all, pick)
    wm_send[0:rank, :] = w_slice
    wm_send[rank:2 * rank, :] = pad_lanes(dot_t(w_all, w_all))
    wm_recv[y] = wm_send[...]

    lane = lax.broadcasted_iota(jnp.int32, (8, 128), 1)
    group = lane // 32
    even = (group == 0) | (group == 2)
    lane_l = lax.broadcasted_iota(jnp.int32, (cube.shape[1] * (cube.shape[2] // 128), 128), 1)
    from_left = lane_l >= 116
    from_right = lane_l < 12
    sy, sx = cube.shape[1], cube.shape[2]
    nb = sx // 128
    vx = nb // nx

    def blur(p):
        rows = dot(table_y[p], cube[p])
        own = jnp.concatenate([rows[:, 128 * b:128 * b + 128] for b in range(nb)], axis=0)
        zero = jnp.zeros((sy, 128), F32)
        left = jnp.concatenate([zero, own[:-sy]], axis=0)
        right = jnp.concatenate([own[sy:], zero], axis=0)
        edge = jnp.where(from_left, left, jnp.where(from_right, right, 0.0))
        out = dot(jnp.concatenate([own, edge], axis=1), table_x[p])
        for q in range(ny):
            for xd in range(nx):
                for h in range(nh):
                    b0 = xd * vx + 2 * h
                    a0 = out[b0 * sy + q * 8:b0 * sy + q * 8 + 8]
                    a1 = out[(b0 + 1) * sy + q * 8:(b0 + 1) * sy + q * 8 + 8]
                    v0 = jnp.where(even, a0, pltpu.roll(a1, 32, 1))
                    v1 = jnp.where(even, pltpu.roll(a0, 96, 1), a1)
                    for cd, v in ((0, v0), (1, v1)):
                        d = (q * nx + xd) * NC + cd
                        send[pl.ds(pl.multiple_of(d * planes * rpp + p * rpp + h * 8, 8), 8), :] = v

    rows_u = planes * rpp
    rows_c = chunk * rpp

    def a2a(j):
        def make(k):
            t = lax.rem(u + k, nu)
            return pltpu.make_async_remote_copy(
                src_ref=send.at[pl.ds(pl.multiple_of(t * rows_u + j * rows_c, 8), rows_c), :],
                dst_ref=recv.at[pl.ds(pl.multiple_of(u * rows_u + j * rows_c, 8), rows_c), :],
                send_sem=a_ss.at[j, k], recv_sem=a_rs.at[j, k], device_id=dev_u(t), device_id_type=MESH)
        return make

    wm = peers(ny, y, dev_y, lambda t: wm_send, wm_recv.at[y], m_ss, m_rs)
    nj = planes // chunk

    @pl.loop(0, nj)
    def _(j):
        for i in range(chunk):
            blur(j * chunk + i)

        @pl.when(j == 0)
        def _():
            pl.semaphore_wait(barrier, nu + nz - 2)
            start(ny, wm)

        start(nu, a2a(j))

    mine = pl.ds(pl.multiple_of(u * rows_u, 8), rows_u)
    recv[mine, :] = send[mine, :]

    wait_recv(ny, wm)

    @pl.loop(0, nj)
    def _(j):
        wait_recv(nu, a2a(j))

    w_z = jnp.concatenate([wm_recv[b][0:rank, 0:pb] for b in range(ny)], axis=1)
    gram_w = sum(wm_recv[b][rank:2 * rank, 0:rank] for b in range(ny))

    def x_of(s):
        return jnp.concatenate([recv[pl.ds(h * 8 + s, ptot, stride=rpp), :] for h in range(nh)], axis=1)

    parts = [dot(w_z, x_of(s)) for s in range(8)]
    lane_r = lax.broadcasted_iota(jnp.int32, (rank, 128), 1) // 32

    def regroup(blocks, g):
        out = None
        for i, blk in enumerate(blocks):
            moved = blk if i == g else pltpu.roll(blk, (32 * (i - g)) % 128, 1)
            out = moved if out is None else jnp.where(lane_r == i, moved, out)
        return out

    order = (0, 2, 1, 3)
    for h in range(nh):
        for g in range(4):
            for half in range(2):
                blocks = [parts[4 * half + i][:, 128 * h:128 * h + 128] for i in range(4)]
                rs_send[4 * h + order[g], :, 128 * half:128 * half + 128] = regroup(blocks, g)
    rs = peers(nz, z, dev_z, lambda t: rs_send.at[t], rs_recv.at[z], z_ss, z_rs)
    start(nz, rs)
    rs_recv[z] = rs_send[z]
    h_rows = h_in[pl.ds(y * 8, 8), :, :].reshape(256, rank)
    h_own = h_rows.T
    denom_h = dot(gram_w, h_own)
    wait_recv(nz, rs)
    numer_h = rs_recv[0]
    for i in range(1, nz):
        numer_h = numer_h + rs_recv[i]
    h_next = h_own * numer_h / denom_h
    hz_send[...] = h_next
    hz = peers(nz, z, dev_z, lambda t: hz_send, hz_recv.at[z], g_ss, g_rs)
    hy = peers(ny, y, dev_y, lambda t: hz_send, hy_recv.at[y], y_ss, y_rs)
    start(nz, hz)
    start(ny, hy)
    hz_recv[z] = h_next
    hy_recv[y] = h_next
    wait_recv(nz, hz)

    hs = []
    for s in range(8):
        half, i = s // 4, s % 4
        cols = []
        for h in range(nh):
            blocks = [hz_recv[4 * h + order[g], :, 128 * half:128 * half + 128] for g in range(4)]
            cols.append(regroup(blocks, i))
        hs.append(jnp.concatenate(cols, axis=1))
    numer_w = None
    gram_h = None
    for s in range(8):
        a = dot_t(x_of(s), hs[s])
        b = dot_t(hs[s], hs[s])
        numer_w = a if numer_w is None else numer_w + a
        gram_h = b if gram_h is None else gram_h + b
    gram_h = pad_lanes(gram_h)
    for b in range(ny):
        wy_send[b, 0:rank, :] = pad_lanes(numer_w[b * pb:(b + 1) * pb].T)
        wy_send[b, rank:2 * rank, :] = gram_h
    wy = peers(ny, y, dev_y, lambda t: wy_send.at[t], wy_recv.at[y], wy_ss, wy_rs)
    start(ny, wy)
    wy_recv[y] = wy_send[y]
    wait_recv(ny, wy)
    total = wy_recv[0]
    for i in range(1, ny):
        total = total + wy_recv[i]
    wx_send[...] = total
    wx = peers(nxc, xc, dev_xc, lambda t: wx_send, wx_recv.at[xc], wx_ss, wx_rs)
    start(nxc, wx)
    wx_recv[xc] = total

    wait_recv(ny, hy)
    for q in range(ny):
        h_out[8 * q:8 * q + 8] = hy_recv[q].T.reshape(8, 32, rank)

    wait_recv(nxc, wx)
    total = wx_recv[0]
    for i in range(1, nxc):
        total = total + wx_recv[i]
    denom_w = dot(total[rank:2 * rank, 0:rank], w_slice)
    w_new = w_slice * total[0:rank] / denom_w
    wz_send[...] = w_new
    wz = peers(nz, z, dev_z, lambda t: wz_send, wz_recv.at[z], wz_ss, wz_rs)
    start(nz, wz)
    wz_recv[z] = w_new
    wait_recv(nz, wz)
    pieces = []
    for xd in range(nx):
        for zd in range(nz):
            pieces.append(wz_recv[zd][:, xd * zs:(xd + 1) * zs])
    w_out[...] = jnp.concatenate(pieces, axis=1)

    @pl.loop(0, nj)
    def _(j):
        wait_send(nu, a2a(j))
    for n, m in ((ny, wm), (nz, rs), (nz, hz), (ny, hy), (ny, wy), (nxc, wx), (nz, wz)):
        wait_send(n, m)


def local(nx, ny, nz, cube, taps_x, taps_y, factor_w, factor_h):
    _, planes, sy, sx = cube.shape
    rank = factor_w.shape[2]
    table_x = column_table(normalized(taps_x[0]))
    table_y = row_table(normalized(taps_y[0]), sy)
    w_t = factor_w[0].T
    h_t = factor_h.transpose(1, 2, 0)
    chunk = 3
    nj = planes // chunk
    nxc = nx * NC
    nu = ny * nxc
    rows = nu * planes * (nz // 4) * 8
    vmem = pl.BlockSpec(memory_space=pltpu.VMEM)
    dma = pltpu.SemaphoreType.DMA
    w_next, h_next = pl.pallas_call(
        functools.partial(kernel, (nx, ny, nz, planes, chunk)),
        out_shape=(jax.ShapeDtypeStruct(w_t.shape, F32), jax.ShapeDtypeStruct(h_t.shape, F32)),
        in_specs=[vmem] * 5,
        out_specs=(vmem, vmem),
        scratch_shapes=[
            pltpu.VMEM((rows, 128), F32), pltpu.VMEM((rows, 128), F32),
            pltpu.VMEM((2 * rank, 128), F32), pltpu.VMEM((ny, 2 * rank, 128), F32),
            pltpu.VMEM((nz, rank, 256), F32), pltpu.VMEM((nz, rank, 256), F32),
            pltpu.VMEM((rank, 256), F32), pltpu.VMEM((nz, rank, 256), F32), pltpu.VMEM((ny, rank, 256), F32),
            pltpu.VMEM((ny, 2 * rank, 128), F32), pltpu.VMEM((ny, 2 * rank, 128), F32),
            pltpu.VMEM((2 * rank, 128), F32), pltpu.VMEM((nxc, 2 * rank, 128), F32),
            pltpu.VMEM((rank, 128), F32), pltpu.VMEM((nz, rank, 128), F32),
            dma((nj, nu)), dma((nj, nu)), dma((ny,)), dma((ny,)), dma((nz,)), dma((nz,)),
            dma((nz,)), dma((nz,)), dma((ny,)), dma((ny,)),
            dma((ny,)), dma((ny,)), dma((nxc,)), dma((nxc,)), dma((nz,)), dma((nz,)),
        ],
        compiler_params=pltpu.CompilerParams(collective_id=0, has_side_effects=True, vmem_limit_bytes=60 << 20),
        name="nmf",
    )(cube[0], table_x, table_y, w_t, h_t)
    return w_next.T[None], h_next.transpose(2, 0, 1)


def solution(mesh):
    n_sp, ny = mesh.shape["sp"], mesh.shape["bd"]
    nx, nz = (4, 8) if n_sp == 64 else (1, n_sp // NC)
    in_specs = (
        P("bd", "sp", None, None),
        P("bd", "sp", None),
        P("bd", "sp", None),
        P("bd", None, None),
        P(None, None, "sp"),
    )
    out_specs = (P("bd", None, None), P(None, None, "sp"))
    return jax.shard_map(functools.partial(local, nx, ny, nz), mesh=mesh, in_specs=in_specs, out_specs=out_specs, check_vma=False)
```

```python
import functools

import jax
import jax.numpy as jnp
from jax import lax
from jax.experimental import pallas as pl
from jax.experimental.pallas import tpu as pltpu
from jax.sharding import PartitionSpec as P

HI = lax.Precision.HIGHEST
MESH = pl.DeviceIdType.MESH
NC = 2
VL = 60
F32 = jnp.float32
ORDER = (0, 2, 1, 3)
ROWS = ((1,), (0,))
LANES = ((1,), (1,))


def dot(a, b, dims=ROWS):
    return lax.dot_general(a, b, (dims, ((), ())), precision=HI, preferred_element_type=F32)


def dot_t(a, b):
    return dot(a, b, LANES)


def split(a):
    high = a.astype(jnp.bfloat16)
    return high, (a - high.astype(F32)).astype(jnp.bfloat16)


def dot3(a, b, dims=ROWS):
    (ah, al), (bh, bl) = split(a), split(b)

    def one(p, q):
        return lax.dot_general(p, q, (dims, ((), ())), preferred_element_type=F32)

    return one(ah, bh) + (one(ah, bl) + one(al, bh))


def pad_lanes(a):
    if a.shape[1] == 128:
        return a
    return jnp.concatenate([a, jnp.zeros((a.shape[0], 128 - a.shape[1]), F32)], axis=1)


def kernel(geo, cube_hbm, taps_x, taps_y, w_hbm, h_hbm, w_out, h_out,
           cube, w_t, h_in, send, recv, wm_send, wm_recv, rs_send, rs_recv, hz_send, hz_recv, hy_recv,
           wc_send, wc_recv, wy_send, wy_recv, wx_send, wx_recv, wz_send, wz_recv,
           cube_sem, in_sem, a_ss, a_rs, m_ss, m_rs, z_ss, z_rs, g_ss, g_rs, y_ss, y_rs,
           wc_ss, wc_rs, wy_ss, wy_rs, wx_ss, wx_rs, wz_ss, wz_rs, wp_ss, wp_rs):
    nx, ny, nz, planes = geo
    nh = nz // 4
    nxc = nx * NC
    nu = ny * nxc
    pb = nxc * planes
    ptot = ny * pb
    zs = NC * planes
    rpu = planes * nh
    ks = nu * rpu
    chunk = 8 // nh
    nj = planes // chunk
    rank = w_t.shape[0]
    half = rank // 2
    sy, sx = cube.shape[1], cube.shape[2]
    sp = lax.axis_index("sp")
    y = lax.axis_index("bd")
    c = lax.rem(sp, NC)
    z = lax.rem(sp // NC, nz)
    x = sp // (NC * nz)
    xc = x * NC + c
    u = y * nxc + xc

    for p in range(planes):
        pltpu.make_async_copy(cube_hbm.at[p], cube.at[p], cube_sem.at[p]).start()
    w_copy = pltpu.make_async_copy(w_hbm, w_t, in_sem.at[0])
    w_copy.start()
    h_copy = pltpu.make_async_copy(h_hbm.at[pl.ds(y * 8, 8)], h_in, in_sem.at[1])
    h_copy.start()

    def dev_u(t):
        tx = lax.rem(t, nxc)
        return (((tx // NC) * nz + z) * NC + lax.rem(tx, NC), t // nxc)

    def dev_z(t):
        return ((x * nz + t) * NC + c, y)

    def dev_y(t):
        return (sp, t)

    def dev_x(t):
        return ((t * nz + z) * NC + c, y)

    partner = (sp + 1 - 2 * c, y)

    barrier = pltpu.get_barrier_semaphore()

    @pl.loop(1, nu)
    def _(k):
        pl.semaphore_signal(barrier, inc=1, device_id=dev_u(lax.rem(u + k, nu)), device_id_type=MESH)

    @pl.loop(1, nz)
    def _(k):
        pl.semaphore_signal(barrier, inc=1, device_id=dev_z(lax.rem(z + k, nz)), device_id_type=MESH)

    def remote(src, dst, ss, rs, dev):
        return pltpu.make_async_remote_copy(src_ref=src, dst_ref=dst, send_sem=ss, recv_sem=rs, device_id=dev, device_id_type=MESH)

    def start(n, me, dev, src, dst, ss, rs):
        @pl.loop(1, n)
        def _(k):
            t = lax.rem(me + k, n)
            remote(src(t), dst, ss, rs, dev(t)).start()

    def wait(ref, sem):
        pltpu.make_async_copy(ref, ref, sem).wait()

    w_copy.wait()
    l_i = lax.broadcasted_iota(jnp.int32, (w_t.shape[1], 128), 0)
    j_i = lax.broadcasted_iota(jnp.int32, (w_t.shape[1], 128), 1)
    xj = jnp.zeros_like(j_i)
    for i in range(1, nx):
        xj = xj + jnp.where(j_i >= zs * i, 1, 0)
    target = xj * (nz * zs) + z * zs + (j_i - zs * xj)
    pick = jnp.where((l_i == target) & (j_i < pb), 1.0, 0.0).astype(F32)
    w_all = w_t[...]
    w_slice = dot(w_all, pick)
    wm_send[0:rank, :] = w_slice
    wm_send[rank:2 * rank, :] = pad_lanes(dot_t(w_all, w_all))
    wm_recv[y] = wm_send[...]

    lane = lax.broadcasted_iota(jnp.int32, (8, 128), 1)
    even = ((lane >= 0) & (lane < 32)) | ((lane >= 64) & (lane < 96))
    nb = sx // 128
    vx = nb // nx
    lane_l = lax.broadcasted_iota(jnp.int32, (sy * nb, 128), 1)
    from_left = lane_l >= 116
    from_right = lane_l < 12
    band_o = lax.broadcasted_iota(jnp.int32, (128, 128), 0)
    band_i = lax.broadcasted_iota(jnp.int32, (128, 128), 1)
    centre = (band_i - band_o < 64) & (band_o - band_i < 64)
    send_flat = send.reshape(8 * ks, 128)

    def band(taps, size):
        t = taps / jnp.sum(taps, axis=1, keepdims=True)
        t = pltpu.roll(jnp.broadcast_to(pad_lanes(t), (size, 128)), 116, 1)
        return pltpu.roll(t, 0, 1, stride=1, stride_axis=0)

    def blur(p):
        rows = dot3(band(taps_y[p], sy)[:, 0:sy], cube[p])
        own = jnp.concatenate([rows[:, 128 * b:128 * b + 128] for b in range(nb)], axis=0)
        zero = jnp.zeros((sy, 128), F32)
        left = jnp.concatenate([zero, own[:-sy]], axis=0)
        right = jnp.concatenate([own[sy:], zero], axis=0)
        edge = jnp.where(from_left, left, jnp.where(from_right, right, 0.0))
        table = band(taps_x[p], 128)
        table = jnp.concatenate([jnp.where(centre, table, 0.0), jnp.where(centre, 0.0, table)], axis=1)
        out = dot3(jnp.concatenate([own, edge], axis=1), table, LANES)
        for q in range(ny):
            for xd in range(nx):
                for h in range(nh):
                    b0 = xd * vx + 2 * h
                    a0 = out[b0 * sy + q * 8:b0 * sy + q * 8 + 8]
                    a1 = out[(b0 + 1) * sy + q * 8:(b0 + 1) * sy + q * 8 + 8]
                    v0 = jnp.where(even, a0, pltpu.roll(a1, 32, 1))
                    v1 = jnp.where(even, pltpu.roll(a0, 96, 1), a1)
                    for cd, v in ((0, v0), (1, v1)):
                        d = (q * nx + xd) * NC + cd
                        send_flat[pl.ds(d * rpu + p * nh + h, 8, stride=ks), :] = v

    def offsets():
        steps = [(dx, dy) for dx in range(nx) for dy in range(ny) if (dx, dy) != (0, 0)]
        steps.sort(key=lambda d: -(min(d[0], nx - d[0]) + min(d[1], ny - d[1])))
        return [(dx, dy, dc) for dx, dy in steps for dc in range(NC)] + [(0, 0, 1)]

    def a2a(k0, nk, row, rows, sem, after=None):
        for i, (dx, dy, dc) in enumerate(offsets()):
            tx, ty, tc = lax.rem(x + dx, nx), lax.rem(y + dy, ny), lax.rem(c + dc, NC)
            t = (ty * nx + tx) * NC + tc
            if after is not None:
                wait(recv.at[0:after, 0:rpu, :], a_ss.at[sem - 1, i])
            remote(send.at[pl.ds(k0, nk), pl.ds(pl.multiple_of(t * rpu + row, 8), rows), :],
                   recv.at[pl.ds(k0, nk), pl.ds(pl.multiple_of(u * rpu + row, 8), rows), :],
                   a_ss.at[sem, i], a_rs.at[sem], ((tx * nz + z) * NC + tc, ty)).start()

    @pl.loop(0, nj)
    def _(j):
        for i in range(chunk):
            p = j * chunk + i
            pltpu.make_async_copy(cube_hbm.at[p], cube.at[p], cube_sem.at[p]).wait()
        for i in range(chunk):
            blur(j * chunk + i)

        @pl.when(j == 0)
        def _():
            pl.semaphore_wait(barrier, nu + nz - 2)
            start(ny, y, dev_y, lambda t: wm_send, wm_recv.at[y], m_ss, m_rs)

        a2a(0, 4, j * 8, 8, 0)

    mine = pl.ds(pl.multiple_of(u * rpu, 8), rpu)
    recv[:, mine, :] = send[:, mine, :]

    wait(wm_recv.at[0:ny - 1], m_rs)
    w_z = jnp.concatenate([wm_recv[b][0:rank, 0:pb] for b in range(ny)], axis=1)
    gram_w = sum(wm_recv[b][rank:2 * rank, 0:rank] for b in range(ny))
    h_copy.wait()
    h_own = h_in[...].reshape(256, rank).T
    denom = dot(gram_w, h_own)

    def packed(a, q):
        return jnp.concatenate([a[0:half, 64 * q:64 * q + 64], a[half:rank, 64 * q:64 * q + 64]], axis=1)

    def regroup(blocks, g):
        lane_r = lax.broadcasted_iota(jnp.int32, (half, 128), 1)
        out = None
        for i, blk in enumerate(blocks):
            moved = blk if i == g else pltpu.roll(blk, (32 * (i - g)) % 128, 1)
            out = moved if out is None else jnp.where(lane_r >= 32 * i, moved, out)
        return out

    def x_of(s):
        return jnp.concatenate([recv[s, pl.ds(h, ptot, stride=nh), :] for h in range(nh)], axis=1)

    peers_z = (nz, z, dev_z)

    def contract(q):
        parts = [dot(w_z, x_of(2 * q + i)) for i in range(2)]
        for h in range(nh):
            cols = [p[:, 128 * h:128 * h + 128] for p in parts]
            blocks = [cols[0][0:half], cols[1][0:half], cols[0][half:rank], cols[1][half:rank]]
            for g in range(4):
                rs_send[q, 4 * h + ORDER[g]] = regroup(blocks, g)
        start(*peers_z, lambda t: rs_send.at[q, t], rs_recv.at[q, z], z_ss.at[q], z_rs.at[q])
        rs_recv[q, z] = rs_send[q, z]

    def update(q):
        wait(rs_recv.at[q, 0:nz - 1], z_rs.at[q])
        numer = rs_recv[q, 0]
        for i in range(1, nz):
            numer = numer + rs_recv[q, i]
        h_next = packed(h_own, q) * numer / packed(denom, q)
        hz_send[q] = h_next
        start(*peers_z, lambda t: hz_send.at[q], hz_recv.at[q, z], g_ss.at[q], g_rs.at[q])
        start(ny, y, dev_y, lambda t: hz_send.at[q], hy_recv.at[q, y], y_ss.at[q], y_rs.at[q])
        hz_recv[q, z] = h_next
        hy_recv[q, y] = h_next

    def gather(q, sums):
        wait(hz_recv.at[q, 0:nz - 1], g_rs.at[q])
        for i in range(2):
            cols = []
            for h in range(nh):
                blocks = [hz_recv[q, 4 * h + ORDER[g]] for g in range(4)]
                cols.append(jnp.concatenate([regroup(blocks, i), regroup(blocks, 2 + i)], axis=0))
            h_s = jnp.concatenate(cols, axis=1)
            new = (dot_t(x_of(2 * q + i), h_s), dot_t(h_s, h_s))
            sums = new if sums is None else (sums[0] + new[0], sums[1] + new[1])
        return sums

    first_half = recv.at[0:4, 0:(nu - 1) * rpu, :]
    quarter = recv.at[0:2, 0:(nu - 1) * rpu, :]
    a2a(4, 2, 0, rpu, 1, after=4)
    wait(first_half, a_rs.at[0])
    contract(0)
    contract(1)
    a2a(6, 2, 0, rpu, 2, after=2)
    wait(quarter, a_rs.at[1])
    contract(2)
    update(0)
    update(1)
    wait(quarter, a_rs.at[2])
    contract(3)
    update(2)
    sums = gather(0, None)
    sums = gather(1, sums)
    for i in range(nu - 1):
        wait(recv.at[0:2, 0:rpu, :], a_ss.at[2, i])
    update(3)
    sums = gather(2, sums)
    for q in range(3):
        wait(rs_recv.at[q, 0:nz - 1], z_ss.at[q])
        wait(hz_recv.at[q, 0:nz - 1], g_ss.at[q])
        wait(hy_recv.at[q, 0:ny - 1], y_ss.at[q])
    wait(wm_recv.at[0:ny - 1], m_ss)
    sums = gather(3, sums)
    numer_w, gram_h = sums

    for f in range(2):
        g_half = gram_h[f * half:(f + 1) * half]
        tail = pad_lanes(jnp.concatenate([g_half[8 * i:8 * i + 8, 32:48] for i in range(3)], axis=1))
        for b in range(ny):
            num = numer_w[b * pb:(b + 1) * pb].T[f * half:(f + 1) * half]
            wc_send[f, b, 0:half, :] = pad_lanes(jnp.concatenate([num, g_half[:, 0:32]], axis=1))
            wc_send[f, b, half:half + 8, :] = tail
    remote(wc_send.at[1 - c], wc_recv, wc_ss, wc_rs, partner).start()
    wait(wc_recv, wc_rs)
    wy_send[...] = wc_send[c] + wc_recv[...]
    start(ny, y, dev_y, lambda t: wy_send.at[t], wy_recv.at[y], wy_ss, wy_rs)
    wy_recv[y] = wy_send[y]

    for q in range(4):
        wait(hy_recv.at[q, 0:ny - 1], y_rs.at[q])
    for b in range(ny):
        cols = []
        for q in range(4):
            v = hy_recv[q, b]
            cols.append(jnp.concatenate([v[:, 0:64], v[:, 64:128]], axis=0))
        h_out[8 * b:8 * b + 8] = jnp.concatenate(cols, axis=1).T.reshape(8, 32, rank)

    wait(wy_recv.at[0:ny - 1], wy_rs)
    total = wy_recv[0]
    for i in range(1, ny):
        total = total + wy_recv[i]
    if nx > 1:
        wx_send[...] = total
        start(nx, x, dev_x, lambda t: wx_send, wx_recv.at[x], wx_ss, wx_rs)
        wx_recv[x] = total
        wait(wx_recv.at[0:nx - 1], wx_rs)
        total = wx_recv[0]
        for i in range(1, nx):
            total = total + wx_recv[i]
    last = total[half:half + 8]
    g_rows = jnp.concatenate([total[0:half, pb:pb + 32],
                              jnp.concatenate([last[:, 16 * i:16 * i + 16] for i in range(3)], axis=0)], axis=1)
    denom_w = dot(g_rows, wm_send[0:rank, :])
    denom_w = jnp.where(lax.broadcasted_iota(jnp.int32, (half, 128), 1) < pb, denom_w, 1.0)
    w_new = wm_send[pl.ds(pl.multiple_of(c * half, 8), half), :] * total[0:half] / denom_w
    mine_w = pl.ds(pl.multiple_of(c * half, 8), half)
    wz_send[...] = w_new
    start(*peers_z, lambda t: wz_send, wz_recv.at[z, mine_w, :], wz_ss, wz_rs)
    wz_recv[z, mine_w, :] = w_new
    wait(wz_recv.at[0:nz - 1, 0:half, :], wz_rs)
    share = remote(wz_recv.at[:, mine_w, :], wz_recv.at[:, mine_w, :], wp_ss, wp_rs, partner)
    share.start()
    wait(rs_recv.at[3, 0:nz - 1], z_ss.at[3])
    wait(hz_recv.at[3, 0:nz - 1], g_ss.at[3])
    wait(hy_recv.at[3, 0:ny - 1], y_ss.at[3])
    wait(wc_recv, wc_ss)
    wait(wy_recv.at[0:ny - 1], wy_ss)
    if nx > 1:
        wait(wx_recv.at[0:nx - 1], wx_ss)
    wait(wz_recv.at[0:nz - 1, 0:half, :], wz_ss)
    share.wait()
    pieces = []
    for xd in range(nx):
        for zd in range(nz):
            pieces.append(wz_recv[zd][:, xd * zs:(xd + 1) * zs])
    w_out[...] = jnp.concatenate(pieces, axis=1)


def local(nx, ny, nz, cube, taps_x, taps_y, factor_w, factor_h):
    _, planes, sy, sx = cube.shape
    rank = factor_w.shape[2]
    w_t = factor_w[0].T
    h_t = factor_h.transpose(1, 2, 0)
    half = rank // 2
    nu = ny * nx * NC
    ks = nu * planes * (nz // 4)
    vmem = pl.BlockSpec(memory_space=pltpu.VMEM)
    anywhere = pl.BlockSpec(memory_space=pltpu.HBM)
    sem = pltpu.SemaphoreType.DMA

    def buf(*shape):
        return pltpu.VMEM(shape, F32)

    w_next, h_next = pl.pallas_call(
        functools.partial(kernel, (nx, ny, nz, planes)),
        out_shape=(buf(*w_t.shape), buf(*h_t.shape)),
        in_specs=[anywhere, vmem, vmem, anywhere, anywhere],
        out_specs=(vmem, vmem),
        scratch_shapes=[
            buf(planes, sy, sx), buf(*w_t.shape), buf(8, 32, rank),
            buf(8, ks, 128), buf(8, ks, 128), buf(2 * rank, 128), buf(ny, 2 * rank, 128),
            buf(4, nz, half, 128), buf(4, nz, half, 128), buf(4, half, 128), buf(4, nz, half, 128), buf(4, ny, half, 128),
            buf(2, ny, half + 8, 128), buf(ny, half + 8, 128), buf(ny, half + 8, 128), buf(ny, half + 8, 128),
            buf(half + 8, 128), buf(nx, half + 8, 128), buf(half, 128), buf(nz, rank, 128),
            sem((planes,)), sem((2,)), sem((3, nu)), sem((3,)), sem, sem, sem((4,)), sem((4,)), sem((4,)), sem((4,)), sem((4,)), sem((4,)),
            sem, sem, sem, sem, sem, sem, sem, sem, sem, sem,
        ],
        compiler_params=pltpu.CompilerParams(collective_id=0, has_side_effects=True, vmem_limit_bytes=VL << 20),
        name="nmf",
    )(cube[0], taps_x.reshape(planes, 1, -1), taps_y.reshape(planes, 1, -1), w_t, h_t)
    return w_next.T[None], h_next.transpose(2, 0, 1)


def solution(mesh):
    n_sp, ny = mesh.shape["sp"], mesh.shape["bd"]
    nx, nz = (4, 8) if n_sp == 64 else (1, n_sp // NC)
    in_specs = (
        P("bd", "sp", None, None),
        P("bd", "sp", None),
        P("bd", "sp", None),
        P("bd", None, None),
        P(None, None, "sp"),
    )
    out_specs = (P("bd", None, None), P(None, None, "sp"))
    return jax.shard_map(functools.partial(local, nx, ny, nz), mesh=mesh, in_specs=in_specs, out_specs=out_specs, check_vma=False)
```

```python
import functools

import jax
import jax.numpy as jnp
from jax import lax
from jax.experimental import pallas as pl
from jax.experimental.pallas import tpu as pltpu
from jax.sharding import PartitionSpec as P

HI = lax.Precision.HIGHEST
MESH = pl.DeviceIdType.MESH
NC = 2
VL = 60
F32 = jnp.float32
ORDER = (0, 2, 1, 3)
ROWS = ((1,), (0,))
LANES = ((1,), (1,))


def dot(a, b, dims=ROWS):
    return lax.dot_general(a, b, (dims, ((), ())), precision=HI, preferred_element_type=F32)


def dot_t(a, b):
    return dot(a, b, LANES)


def split(a):
    high = a.astype(jnp.bfloat16)
    return high, (a - high.astype(F32)).astype(jnp.bfloat16)


def dot3(a, b, dims=ROWS):
    (ah, al), (bh, bl) = split(a), split(b)

    def one(p, q):
        return lax.dot_general(p, q, (dims, ((), ())), preferred_element_type=F32)

    return one(ah, bh) + (one(ah, bl) + one(al, bh))


def pad_lanes(a):
    if a.shape[1] == 128:
        return a
    return jnp.concatenate([a, jnp.zeros((a.shape[0], 128 - a.shape[1]), F32)], axis=1)


def kernel(geo, cube_hbm, tx_hbm, ty_hbm, w_hbm, h_hbm, w_out, h_out,
           cube, taps_x, taps_y, w_t, h_in, send, recv, wm_send, wm_recv, rs_send, rs_recv, hz_send, hz_recv, hy_recv,
           wc_send, wc_recv, wy_send, wy_recv, wx_send, wx_recv, wz_send, wz_recv,
           cube_sem, in_sem, a_ss, a_rs, m_ss, m_rs, z_ss, z_rs, g_ss, g_rs, y_ss, y_rs,
           wc_ss, wc_rs, wy_ss, wy_rs, wx_ss, wx_rs, wz_ss, wz_rs, wp_ss, wp_rs):
    nx, ny, nz, planes = geo
    nh = nz // 4
    nxc = nx * NC
    nu = ny * nxc
    pb = nxc * planes
    ptot = ny * pb
    zs = NC * planes
    rpu = planes * nh
    ks = nu * rpu
    chunk = 8 // nh
    nj = planes // chunk
    rank = w_t.shape[0]
    half = rank // 2
    sy, sx = cube.shape[1], cube.shape[2]
    sp = lax.axis_index("sp")
    y = lax.axis_index("bd")
    c = lax.rem(sp, NC)
    z = lax.rem(sp // NC, nz)
    x = sp // (NC * nz)
    xc = x * NC + c
    u = y * nxc + xc

    def dev_z(t):
        return ((x * nz + t) * NC + c, y)

    def dev_y(t):
        return (sp, t)

    def dev_x(t):
        return ((t * nz + z) * NC + c, y)

    partner = (sp + 1 - 2 * c, y)

    barrier = pltpu.get_barrier_semaphore()

    def offsets():
        rounds = ((1, 1), (3, 3), (0, 2), (2, 0), (1, 3), (3, 1), (2, 2), (1, 2), (3, 0), (0, 1), (2, 3), (1, 0), (3, 2), (0, 3), (2, 1))
        steps = [d for d in rounds if d[0] < nx and d[1] < ny]
        return [(dx, dy, dc) for dc in range(NC) for dx, dy in steps] + [(0, 0, 1)]

    for dx, dy, dc in offsets():
        there = ((lax.rem(x + dx, nx) * nz + z) * NC + lax.rem(c + dc, NC), lax.rem(y + dy, ny))
        pl.semaphore_signal(barrier, inc=1, device_id=there, device_id_type=MESH)
    for dz in range(1, nz):
        pl.semaphore_signal(barrier, inc=1, device_id=dev_z(lax.rem(z + dz, nz)), device_id_type=MESH)

    tx_copy = pltpu.make_async_copy(tx_hbm, taps_x, in_sem.at[2])
    tx_copy.start()
    ty_copy = pltpu.make_async_copy(ty_hbm, taps_y, in_sem.at[3])
    ty_copy.start()
    for p in range(planes):
        pltpu.make_async_copy(cube_hbm.at[p], cube.at[p], cube_sem.at[p]).start()
    w_copy = pltpu.make_async_copy(w_hbm, w_t, in_sem.at[0])
    w_copy.start()
    h_copy = pltpu.make_async_copy(h_hbm.at[pl.ds(y * 8, 8)], h_in, in_sem.at[1])
    h_copy.start()

    def remote(src, dst, ss, rs, dev):
        return pltpu.make_async_remote_copy(src_ref=src, dst_ref=dst, send_sem=ss, recv_sem=rs, device_id=dev, device_id_type=MESH)

    def start(n, me, dev, src, dst, ss, rs):
        @pl.loop(1, n)
        def _(k):
            t = lax.rem(me + k, n)
            remote(src(t), dst, ss, rs, dev(t)).start()

    def wait(ref, sem):
        pltpu.make_async_copy(ref, ref, sem).wait()

    lane = lax.broadcasted_iota(jnp.int32, (8, 128), 1)
    even = ((lane >= 0) & (lane < 32)) | ((lane >= 64) & (lane < 96))
    nb = sx // 128
    vx = nb // nx
    lane_l = lax.broadcasted_iota(jnp.int32, (sy * nb, 128), 1)
    from_left = lane_l >= 116
    from_right = lane_l < 12
    band_o = lax.broadcasted_iota(jnp.int32, (128, 128), 0)
    band_i = lax.broadcasted_iota(jnp.int32, (128, 128), 1)
    centre = (band_i - band_o < 64) & (band_o - band_i < 64)
    send_flat = send.reshape(8 * ks, 128)

    def band(taps, size):
        t = taps / jnp.sum(taps, axis=1, keepdims=True)
        t = pltpu.roll(jnp.broadcast_to(pad_lanes(t), (size, 128)), 116, 1)
        return pltpu.roll(t, 0, 1, stride=1, stride_axis=0)

    def blur(p):
        rows = dot3(band(taps_y[p], sy)[:, 0:sy], cube[p])
        own = jnp.concatenate([rows[:, 128 * b:128 * b + 128] for b in range(nb)], axis=0)
        zero = jnp.zeros((sy, 128), F32)
        left = jnp.concatenate([zero, own[:-sy]], axis=0)
        right = jnp.concatenate([own[sy:], zero], axis=0)
        edge = jnp.where(from_left, left, jnp.where(from_right, right, 0.0))
        table = band(taps_x[p], 128)
        table = jnp.concatenate([jnp.where(centre, table, 0.0), jnp.where(centre, 0.0, table)], axis=1)
        out = dot3(jnp.concatenate([own, edge], axis=1), table, LANES)
        for q in range(ny):
            for xd in range(nx):
                for h in range(nh):
                    b0 = xd * vx + 2 * h
                    a0 = out[b0 * sy + q * 8:b0 * sy + q * 8 + 8]
                    a1 = out[(b0 + 1) * sy + q * 8:(b0 + 1) * sy + q * 8 + 8]
                    v0 = jnp.where(even, a0, pltpu.roll(a1, 32, 1))
                    v1 = jnp.where(even, pltpu.roll(a0, 96, 1), a1)
                    for cd, v in ((0, v0), (1, v1)):
                        d = (q * nx + xd) * NC + cd
                        send_flat[pl.ds(d * 8 * rpu + p * nh + h, 8, stride=rpu), :] = v

    def a2a(k0, nk, row, rows, sem, after=None):
        for i, (dx, dy, dc) in enumerate(offsets()):
            tx, ty, tc = lax.rem(x + dx, nx), lax.rem(y + dy, ny), lax.rem(c + dc, NC)
            t = (ty * nx + tx) * NC + tc
            if after is not None:
                wait(recv.at[0:after, 0:rpu, :], a_ss.at[sem - 1, i])
            remote(send.at[pl.ds(t * 8 + k0, nk), pl.ds(row, rows), :],
                   recv.at[pl.ds(k0, nk), pl.ds(pl.multiple_of(u * rpu + row, 8), rows), :],
                   a_ss.at[sem, i], a_rs.at[sem], ((tx * nz + z) * NC + tc, ty)).start()

    tx_copy.wait()
    ty_copy.wait()

    @pl.loop(0, nj)
    def _(j):
        for i in range(chunk):
            p = j * chunk + i
            pltpu.make_async_copy(cube_hbm.at[p], cube.at[p], cube_sem.at[p]).wait()
        for i in range(chunk):
            blur(j * chunk + i)

        @pl.when(j == 0)
        def _():
            w_copy.wait()
            l_i = lax.broadcasted_iota(jnp.int32, (w_t.shape[1], 128), 0)
            j_i = lax.broadcasted_iota(jnp.int32, (w_t.shape[1], 128), 1)
            xj = jnp.zeros_like(j_i)
            for i in range(1, nx):
                xj = xj + jnp.where(j_i >= zs * i, 1, 0)
            target = xj * (nz * zs) + z * zs + (j_i - zs * xj)
            pick = jnp.where((l_i == target) & (j_i < pb), 1.0, 0.0).astype(F32)
            w_all = w_t[...]
            w_slice = dot(w_all, pick)
            wm_send[0:rank, :] = w_slice
            wm_send[rank:2 * rank, :] = pad_lanes(dot_t(w_all, w_all))
            wm_recv[y] = wm_send[...]
            pl.semaphore_wait(barrier, nu + nz - 2)
            start(ny, y, dev_y, lambda t: wm_send, wm_recv.at[y], m_ss, m_rs)

        a2a(0, 4, pl.multiple_of(j * 8, 8), 8, 0)

    mine = pl.ds(pl.multiple_of(u * rpu, 8), rpu)
    for k in range(8):
        recv[k, mine, :] = send[u * 8 + k]

    def packed(a, q):
        return jnp.concatenate([a[0:half, 64 * q:64 * q + 64], a[half:rank, 64 * q:64 * q + 64]], axis=1)

    def regroup(blocks, g):
        lane_r = lax.broadcasted_iota(jnp.int32, (half, 128), 1)
        out = None
        for i, blk in enumerate(blocks):
            moved = blk if i == g else pltpu.roll(blk, (32 * (i - g)) % 128, 1)
            out = moved if out is None else jnp.where(lane_r >= 32 * i, moved, out)
        return out

    def x_of(s):
        return jnp.concatenate([recv[s, pl.ds(h, ptot, stride=nh), :] for h in range(nh)], axis=1)

    peers_z = (nz, z, dev_z)

    def contract(q):
        parts = [dot(w_z, x_of(2 * q + i)) for i in range(2)]
        for h in range(nh):
            cols = [p[:, 128 * h:128 * h + 128] for p in parts]
            blocks = [cols[0][0:half], cols[1][0:half], cols[0][half:rank], cols[1][half:rank]]
            for g in range(4):
                rs_send[q, 4 * h + ORDER[g]] = regroup(blocks, g)
        start(*peers_z, lambda t: rs_send.at[q, t], rs_recv.at[q, z], z_ss.at[q], z_rs.at[q])
        rs_recv[q, z] = rs_send[q, z]

    def update(q):
        wait(rs_recv.at[q, 0:nz - 1], z_rs.at[q])
        numer = rs_recv[q, 0]
        for i in range(1, nz):
            numer = numer + rs_recv[q, i]
        h_next = packed(h_own, q) * numer / packed(denom, q)
        hz_send[q] = h_next
        start(*peers_z, lambda t: hz_send.at[q], hz_recv.at[q, z], g_ss.at[q], g_rs.at[q])
        start(ny, y, dev_y, lambda t: hz_send.at[q], hy_recv.at[q, y], y_ss.at[q], y_rs.at[q])
        hz_recv[q, z] = h_next
        hy_recv[q, y] = h_next

    def gather(q, sums):
        wait(hz_recv.at[q, 0:nz - 1], g_rs.at[q])
        for i in range(2):
            cols = []
            for h in range(nh):
                blocks = [hz_recv[q, 4 * h + ORDER[g]] for g in range(4)]
                cols.append(jnp.concatenate([regroup(blocks, i), regroup(blocks, 2 + i)], axis=0))
            h_s = jnp.concatenate(cols, axis=1)
            new = (dot_t(x_of(2 * q + i), h_s), dot_t(h_s, h_s))
            sums = new if sums is None else (sums[0] + new[0], sums[1] + new[1])
        return sums

    first_half = recv.at[0:4, 0:(nu - 1) * rpu, :]
    quarter = recv.at[0:2, 0:(nu - 1) * rpu, :]
    a2a(4, 2, 0, rpu, 1, after=4)
    wait(wm_recv.at[0:ny - 1], m_rs)
    w_z = jnp.concatenate([wm_recv[b][0:rank, 0:pb] for b in range(ny)], axis=1)
    gram_w = sum(wm_recv[b][rank:2 * rank, 0:rank] for b in range(ny))
    h_copy.wait()
    h_own = h_in[...].reshape(256, rank).T
    denom = dot(gram_w, h_own)
    wait(first_half, a_rs.at[0])
    contract(0)
    contract(1)
    a2a(6, 2, 0, rpu, 2, after=2)
    wait(quarter, a_rs.at[1])
    contract(2)
    update(0)
    update(1)
    update(2)
    wait(quarter, a_rs.at[2])
    contract(3)
    sums = gather(0, None)
    sums = gather(1, sums)
    for i in range(nu - 1):
        wait(recv.at[0:2, 0:rpu, :], a_ss.at[2, i])
    update(3)
    sums = gather(2, sums)
    for q in range(3):
        wait(rs_recv.at[q, 0:nz - 1], z_ss.at[q])
        wait(hz_recv.at[q, 0:nz - 1], g_ss.at[q])
        wait(hy_recv.at[q, 0:ny - 1], y_ss.at[q])
    wait(wm_recv.at[0:ny - 1], m_ss)
    sums = gather(3, sums)
    numer_w, gram_h = sums

    for f in range(2):
        g_half = gram_h[f * half:(f + 1) * half]
        tail = pad_lanes(jnp.concatenate([g_half[8 * i:8 * i + 8, 32:48] for i in range(3)], axis=1))
        for b in range(ny):
            num = numer_w[b * pb:(b + 1) * pb].T[f * half:(f + 1) * half]
            wc_send[f, b, 0:half, :] = pad_lanes(jnp.concatenate([num, g_half[:, 0:32]], axis=1))
            wc_send[f, b, half:half + 8, :] = tail
    remote(wc_send.at[1 - c], wc_recv, wc_ss, wc_rs, partner).start()
    wait(wc_recv, wc_rs)
    wy_send[...] = wc_send[c] + wc_recv[...]
    start(ny, y, dev_y, lambda t: wy_send.at[t], wy_recv.at[y], wy_ss, wy_rs)
    wy_recv[y] = wy_send[y]

    for q in range(4):
        wait(hy_recv.at[q, 0:ny - 1], y_rs.at[q])
    for b in range(ny):
        cols = []
        for q in range(4):
            v = hy_recv[q, b]
            cols.append(jnp.concatenate([v[:, 0:64], v[:, 64:128]], axis=0))
        h_out[8 * b:8 * b + 8] = jnp.concatenate(cols, axis=1).T.reshape(8, 32, rank)

    wait(wy_recv.at[0:ny - 1], wy_rs)
    total = wy_recv[0]
    for i in range(1, ny):
        total = total + wy_recv[i]
    if nx > 1:
        wx_send[...] = total
        start(nx, x, dev_x, lambda t: wx_send, wx_recv.at[x], wx_ss, wx_rs)
        wx_recv[x] = total
        wait(wx_recv.at[0:nx - 1], wx_rs)
        total = wx_recv[0]
        for i in range(1, nx):
            total = total + wx_recv[i]
    last = total[half:half + 8]
    g_rows = jnp.concatenate([total[0:half, pb:pb + 32],
                              jnp.concatenate([last[:, 16 * i:16 * i + 16] for i in range(3)], axis=0)], axis=1)
    denom_w = dot(g_rows, wm_send[0:rank, :])
    denom_w = jnp.where(lax.broadcasted_iota(jnp.int32, (half, 128), 1) < pb, denom_w, 1.0)
    w_new = wm_send[pl.ds(pl.multiple_of(c * half, 8), half), :] * total[0:half] / denom_w
    mine_w = pl.ds(pl.multiple_of(c * half, 8), half)
    wz_send[...] = w_new
    start(*peers_z, lambda t: wz_send, wz_recv.at[z, mine_w, :], wz_ss, wz_rs)
    wz_recv[z, mine_w, :] = w_new
    wait(wz_recv.at[0:nz - 1, 0:half, :], wz_rs)
    share = remote(wz_recv.at[:, mine_w, :], wz_recv.at[:, mine_w, :], wp_ss, wp_rs, partner)
    share.start()
    wait(rs_recv.at[3, 0:nz - 1], z_ss.at[3])
    wait(hz_recv.at[3, 0:nz - 1], g_ss.at[3])
    wait(hy_recv.at[3, 0:ny - 1], y_ss.at[3])
    wait(wc_recv, wc_ss)
    wait(wy_recv.at[0:ny - 1], wy_ss)
    if nx > 1:
        wait(wx_recv.at[0:nx - 1], wx_ss)
    wait(wz_recv.at[0:nz - 1, 0:half, :], wz_ss)
    share.wait()
    pieces = []
    for xd in range(nx):
        for zd in range(nz):
            pieces.append(wz_recv[zd][:, xd * zs:(xd + 1) * zs])
    w_out[...] = jnp.concatenate(pieces, axis=1)


def local(nx, ny, nz, cube, taps_x, taps_y, factor_w, factor_h):
    _, planes, sy, sx = cube.shape
    rank = factor_w.shape[2]
    w_t = factor_w[0].T
    h_t = factor_h.transpose(1, 2, 0)
    half = rank // 2
    nu = ny * nx * NC
    ks = nu * planes * (nz // 4)
    vmem = pl.BlockSpec(memory_space=pltpu.VMEM)
    anywhere = pl.BlockSpec(memory_space=pltpu.HBM)
    sem = pltpu.SemaphoreType.DMA

    def buf(*shape):
        return pltpu.VMEM(shape, F32)

    w_next, h_next = pl.pallas_call(
        functools.partial(kernel, (nx, ny, nz, planes)),
        out_shape=(buf(*w_t.shape), buf(*h_t.shape)),
        in_specs=[anywhere] * 5,
        out_specs=(vmem, vmem),
        scratch_shapes=[
            buf(planes, sy, sx), buf(planes, 1, taps_x.shape[2]), buf(planes, 1, taps_y.shape[2]), buf(*w_t.shape), buf(8, 32, rank),
            buf(8 * nu, ks // nu, 128), buf(8, ks, 128), buf(2 * rank, 128), buf(ny, 2 * rank, 128),
            buf(4, nz, half, 128), buf(4, nz, half, 128), buf(4, half, 128), buf(4, nz, half, 128), buf(4, ny, half, 128),
            buf(2, ny, half + 8, 128), buf(ny, half + 8, 128), buf(ny, half + 8, 128), buf(ny, half + 8, 128),
            buf(half + 8, 128), buf(nx, half + 8, 128), buf(half, 128), buf(nz, rank, 128),
            sem((planes,)), sem((4,)), sem((3, nu)), sem((3,)), sem, sem, sem((4,)), sem((4,)), sem((4,)), sem((4,)), sem((4,)), sem((4,)),
            sem, sem, sem, sem, sem, sem, sem, sem, sem, sem,
        ],
        compiler_params=pltpu.CompilerParams(collective_id=0, has_side_effects=True, vmem_limit_bytes=VL << 20),
        name="nmf",
    )(cube[0], taps_x.reshape(planes, 1, -1), taps_y.reshape(planes, 1, -1), w_t, h_t)
    return w_next.T[None], h_next.transpose(2, 0, 1)


def solution(mesh):
    n_sp, ny = mesh.shape["sp"], mesh.shape["bd"]
    nx, nz = (4, 8) if n_sp == 64 else (1, n_sp // NC)
    in_specs = (
        P("bd", "sp", None, None),
        P("bd", "sp", None),
        P("bd", "sp", None),
        P("bd", None, None),
        P(None, None, "sp"),
    )
    out_specs = (P("bd", None, None), P(None, None, "sp"))
    return jax.shard_map(functools.partial(local, nx, ny, nz), mesh=mesh, in_specs=in_specs, out_specs=out_specs, check_vma=False)
```

```python
import functools

import jax
import jax.numpy as jnp
from jax import lax
from jax.experimental import pallas as pl
from jax.experimental.pallas import tpu as pltpu
from jax.sharding import PartitionSpec as P

HI = lax.Precision.HIGHEST
MESH = pl.DeviceIdType.MESH
NC = 2
VL = 60
F32 = jnp.float32
ORDER = (0, 2, 1, 3)
ROWS = ((1,), (0,))
LANES = ((1,), (1,))


def dot(a, b, dims=ROWS):
    return lax.dot_general(a, b, (dims, ((), ())), precision=HI, preferred_element_type=F32)


def dot_t(a, b):
    return dot(a, b, LANES)


def split(a):
    high = a.astype(jnp.bfloat16)
    return high, (a - high.astype(F32)).astype(jnp.bfloat16)


def dot3(a, b, dims=ROWS):
    (ah, al), (bh, bl) = split(a), split(b)

    def one(p, q):
        return lax.dot_general(p, q, (dims, ((), ())), preferred_element_type=F32)

    return one(ah, bh) + (one(ah, bl) + one(al, bh))


def pad_lanes(a):
    if a.shape[1] == 128:
        return a
    return jnp.concatenate([a, jnp.zeros((a.shape[0], 128 - a.shape[1]), F32)], axis=1)


def kernel(geo, cube_hbm, tx_hbm, ty_hbm, w_hbm, h_hbm, w_out, h_out,
           cube, taps_x, taps_y, w_t, h_in, send, recv, wm_send, wm_recv, rs_send, rs_recv, hz_send, hz_recv, hy_recv,
           wc_send, wy_recv, wx_send, wx_recv, wz_send, wz_recv,
           cube_sem, in_sem, a_ss, a_rs, m_ss, m_rs, z_ss, z_rs, g_ss, g_rs, y_ss, y_rs,
           wy_ss, wy_rs, wx_ss, wx_rs, wz_ss, wz_rs, wp_ss, wp_rs):
    nx, ny, nz, planes = geo
    nh = nz // 4
    nxc = nx * NC
    nu = ny * nxc
    pb = nxc * planes
    ptot = ny * pb
    zs = NC * planes
    rpu = planes * nh
    ks = nu * rpu
    chunk = 8 // nh
    nj = planes // chunk
    rank = w_t.shape[0]
    half = rank // 2
    sy, sx = cube.shape[1], cube.shape[2]
    sp = lax.axis_index("sp")
    y = lax.axis_index("bd")
    c = lax.rem(sp, NC)
    z = lax.rem(sp // NC, nz)
    x = sp // (NC * nz)
    xc = x * NC + c
    u = y * nxc + xc

    def dev_z(t):
        return ((x * nz + t) * NC + c, y)

    def dev_y(t):
        return (sp, t)

    def dev_x(t):
        return ((t * nz + z) * NC + c, y)

    partner = (sp + 1 - 2 * c, y)

    barrier = pltpu.get_barrier_semaphore()

    def offsets():
        steps = [(dx, dy) for dy in (2, 1, 3, 0) for dx in (1, 3, 0, 2) if dx < nx and dy < ny and (dx, dy) != (0, 0)]
        return [(dx, dy, dc) for dc in range(NC) for dx, dy in steps] + [(0, 0, 1)]

    for dx, dy, dc in offsets():
        there = ((lax.rem(x + dx, nx) * nz + z) * NC + lax.rem(c + dc, NC), lax.rem(y + dy, ny))
        pl.semaphore_signal(barrier, inc=1, device_id=there, device_id_type=MESH)
    for dz in range(1, nz):
        pl.semaphore_signal(barrier, inc=1, device_id=dev_z(lax.rem(z + dz, nz)), device_id_type=MESH)

    tx_copy = pltpu.make_async_copy(tx_hbm, taps_x, in_sem.at[2])
    tx_copy.start()
    ty_copy = pltpu.make_async_copy(ty_hbm, taps_y, in_sem.at[3])
    ty_copy.start()
    for p in range(planes):
        pltpu.make_async_copy(cube_hbm.at[p], cube.at[p], cube_sem.at[p]).start()
    w_copy = pltpu.make_async_copy(w_hbm, w_t, in_sem.at[0])
    w_copy.start()
    h_copy = pltpu.make_async_copy(h_hbm.at[pl.ds(y * 8, 8)], h_in, in_sem.at[1])
    h_copy.start()

    def remote(src, dst, ss, rs, dev):
        return pltpu.make_async_remote_copy(src_ref=src, dst_ref=dst, send_sem=ss, recv_sem=rs, device_id=dev, device_id_type=MESH)

    def start(n, me, dev, src, dst, ss, rs):
        @pl.loop(1, n)
        def _(k):
            t = lax.rem(me + k, n)
            remote(src(t), dst, ss, rs, dev(t)).start()

    def wait(ref, sem):
        pltpu.make_async_copy(ref, ref, sem).wait()

    lane = lax.broadcasted_iota(jnp.int32, (8, 128), 1)
    even = ((lane >= 0) & (lane < 32)) | ((lane >= 64) & (lane < 96))
    nb = sx // 128
    vx = nb // nx
    lane_l = lax.broadcasted_iota(jnp.int32, (sy * nb, 128), 1)
    from_left = lane_l >= 116
    from_right = lane_l < 12
    band_o = lax.broadcasted_iota(jnp.int32, (128, 128), 0)
    band_i = lax.broadcasted_iota(jnp.int32, (128, 128), 1)
    centre = (band_i - band_o < 64) & (band_o - band_i < 64)
    send_flat = send.reshape(8 * ks, 128)

    def band(taps, size):
        t = taps / jnp.sum(taps, axis=1, keepdims=True)
        t = pltpu.roll(jnp.broadcast_to(pad_lanes(t), (size, 128)), 116, 1)
        return pltpu.roll(t, 0, 1, stride=1, stride_axis=0)

    def blur(p):
        rows = dot3(band(taps_y[p], sy)[:, 0:sy], cube[p])
        own = jnp.concatenate([rows[:, 128 * b:128 * b + 128] for b in range(nb)], axis=0)
        zero = jnp.zeros((sy, 128), F32)
        left = jnp.concatenate([zero, own[:-sy]], axis=0)
        right = jnp.concatenate([own[sy:], zero], axis=0)
        edge = jnp.where(from_left, left, jnp.where(from_right, right, 0.0))
        table = band(taps_x[p], 128)
        table = jnp.concatenate([jnp.where(centre, table, 0.0), jnp.where(centre, 0.0, table)], axis=1)
        out = dot3(jnp.concatenate([own, edge], axis=1), table, LANES)
        for q in range(ny):
            for xd in range(nx):
                for h in range(nh):
                    b0 = xd * vx + 2 * h
                    a0 = out[b0 * sy + q * 8:b0 * sy + q * 8 + 8]
                    a1 = out[(b0 + 1) * sy + q * 8:(b0 + 1) * sy + q * 8 + 8]
                    v0 = jnp.where(even, a0, pltpu.roll(a1, 32, 1))
                    v1 = jnp.where(even, pltpu.roll(a0, 96, 1), a1)
                    for cd, v in ((0, v0), (1, v1)):
                        d = (q * nx + xd) * NC + cd
                        send_flat[pl.ds(d * 8 * rpu + p * nh + h, 8, stride=rpu), :] = v

    def a2a(k0, nk, row, rows, sem, after=None):
        for i, (dx, dy, dc) in enumerate(offsets()):
            tx, ty, tc = lax.rem(x + dx, nx), lax.rem(y + dy, ny), lax.rem(c + dc, NC)
            t = (ty * nx + tx) * NC + tc
            if after is not None:
                wait(recv.at[0:after, 0:rpu, :], a_ss.at[sem - 1, i])
            remote(send.at[pl.ds(t * 8 + k0, nk), pl.ds(row, rows), :],
                   recv.at[pl.ds(k0, nk), pl.ds(pl.multiple_of(u * rpu + row, 8), rows), :],
                   a_ss.at[sem, i], a_rs.at[sem], ((tx * nz + z) * NC + tc, ty)).start()

    tx_copy.wait()
    ty_copy.wait()

    @pl.loop(0, nj)
    def _(j):
        for i in range(chunk):
            p = j * chunk + i
            pltpu.make_async_copy(cube_hbm.at[p], cube.at[p], cube_sem.at[p]).wait()
        for i in range(chunk):
            blur(j * chunk + i)

        @pl.when(j == 0)
        def _():
            w_copy.wait()
            l_i = lax.broadcasted_iota(jnp.int32, (w_t.shape[1], 128), 0)
            j_i = lax.broadcasted_iota(jnp.int32, (w_t.shape[1], 128), 1)
            xj = jnp.zeros_like(j_i)
            for i in range(1, nx):
                xj = xj + jnp.where(j_i >= zs * i, 1, 0)
            target = xj * (nz * zs) + z * zs + (j_i - zs * xj)
            pick = jnp.where((l_i == target) & (j_i < pb), 1.0, 0.0).astype(F32)
            w_all = w_t[...]
            w_slice = dot(w_all, pick)
            wm_send[0:rank, :] = w_slice
            wm_send[rank:2 * rank, :] = pad_lanes(dot_t(w_all, w_all))
            wm_recv[y] = wm_send[...]
            pl.semaphore_wait(barrier, nu + nz - 2)
            start(ny, y, dev_y, lambda t: wm_send, wm_recv.at[y], m_ss, m_rs)

        a2a(0, 4, pl.multiple_of(j * 8, 8), 8, 0)

    mine = pl.ds(pl.multiple_of(u * rpu, 8), rpu)
    for k in range(8):
        recv[k, mine, :] = send[u * 8 + k]

    def packed(a, q):
        return jnp.concatenate([a[0:half, 64 * q:64 * q + 64], a[half:rank, 64 * q:64 * q + 64]], axis=1)

    def regroup(blocks, g):
        lane_r = lax.broadcasted_iota(jnp.int32, (half, 128), 1)
        out = None
        for i, blk in enumerate(blocks):
            moved = blk if i == g else pltpu.roll(blk, (32 * (i - g)) % 128, 1)
            out = moved if out is None else jnp.where(lane_r >= 32 * i, moved, out)
        return out

    def x_of(s):
        return jnp.concatenate([recv[s, pl.ds(h, ptot, stride=nh), :] for h in range(nh)], axis=1)

    peers_z = (nz, z, dev_z)

    def contract(q):
        parts = [dot(w_z, x_of(2 * q + i)) for i in range(2)]
        for h in range(nh):
            cols = [p[:, 128 * h:128 * h + 128] for p in parts]
            blocks = [cols[0][0:half], cols[1][0:half], cols[0][half:rank], cols[1][half:rank]]
            for g in range(4):
                rs_send[q, 4 * h + ORDER[g]] = regroup(blocks, g)
        start(*peers_z, lambda t: rs_send.at[q, t], rs_recv.at[q, z], z_ss.at[q], z_rs.at[q])
        rs_recv[q, z] = rs_send[q, z]

    def update(q):
        wait(rs_recv.at[q, 0:nz - 1], z_rs.at[q])
        numer = rs_recv[q, 0]
        for i in range(1, nz):
            numer = numer + rs_recv[q, i]
        h_next = packed(h_own, q) * numer / packed(denom, q)
        hz_send[q] = h_next
        start(*peers_z, lambda t: hz_send.at[q], hz_recv.at[q, z], g_ss.at[q], g_rs.at[q])
        start(ny, y, dev_y, lambda t: hz_send.at[q], hy_recv.at[q, y], y_ss.at[q], y_rs.at[q])
        hz_recv[q, z] = h_next
        hy_recv[q, y] = h_next

    def gather(q, sums):
        wait(hz_recv.at[q, 0:nz - 1], g_rs.at[q])
        for i in range(2):
            cols = []
            for h in range(nh):
                blocks = [hz_recv[q, 4 * h + ORDER[g]] for g in range(4)]
                cols.append(jnp.concatenate([regroup(blocks, i), regroup(blocks, 2 + i)], axis=0))
            h_s = jnp.concatenate(cols, axis=1)
            new = (dot_t(x_of(2 * q + i), h_s), dot_t(h_s, h_s))
            sums = new if sums is None else (sums[0] + new[0], sums[1] + new[1])
        return sums

    first_half = recv.at[0:4, 0:(nu - 1) * rpu, :]
    quarter = recv.at[0:2, 0:(nu - 1) * rpu, :]
    a2a(4, 2, 0, rpu, 1, after=4)
    wait(wm_recv.at[0:ny - 1], m_rs)
    w_z = jnp.concatenate([wm_recv[b][0:rank, 0:pb] for b in range(ny)], axis=1)
    gram_w = sum(wm_recv[b][rank:2 * rank, 0:rank] for b in range(ny))
    h_copy.wait()
    h_own = h_in[...].reshape(256, rank).T
    denom = dot(gram_w, h_own)
    wait(first_half, a_rs.at[0])
    contract(0)
    contract(1)
    a2a(6, 2, 0, rpu, 2, after=2)
    wait(quarter, a_rs.at[1])
    contract(2)
    update(0)
    update(1)
    wait(quarter, a_rs.at[2])
    contract(3)
    update(2)
    sums = gather(0, None)
    sums = gather(1, sums)
    for i in range(nu - 1):
        wait(recv.at[0:2, 0:rpu, :], a_ss.at[2, i])
    update(3)
    sums = gather(2, sums)
    for q in range(3):
        wait(rs_recv.at[q, 0:nz - 1], z_ss.at[q])
        wait(hz_recv.at[q, 0:nz - 1], g_ss.at[q])
        wait(hy_recv.at[q, 0:ny - 1], y_ss.at[q])
    wait(wm_recv.at[0:ny - 1], m_ss)
    sums = gather(3, sums)
    numer_w, gram_h = sums

    for f in range(2):
        g_half = gram_h[f * half:(f + 1) * half]
        tail = pad_lanes(jnp.concatenate([g_half[8 * i:8 * i + 8, 32:48] for i in range(3)], axis=1))
        for b in range(ny):
            num = numer_w[b * pb:(b + 1) * pb].T[f * half:(f + 1) * half]
            wc_send[f, b, 0:half, :] = pad_lanes(jnp.concatenate([num, g_half[:, 0:32]], axis=1))
            wc_send[f, b, half:half + 8, :] = tail
    for dc in range(NC):
        tc = lax.rem(c + dc, NC)
        for dy in range(ny):
            ty = lax.rem(y + dy, ny)
            if dy or dc:
                remote(wc_send.at[tc, ty], wy_recv.at[y * NC + c], wy_ss, wy_rs, (sp - c + tc, ty)).start()
    wy_recv[y * NC + c] = wc_send[c, y]

    for q in range(4):
        wait(hy_recv.at[q, 0:ny - 1], y_rs.at[q])
    for b in range(ny):
        cols = []
        for q in range(4):
            v = hy_recv[q, b]
            cols.append(jnp.concatenate([v[:, 0:64], v[:, 64:128]], axis=0))
        h_out[8 * b:8 * b + 8] = jnp.concatenate(cols, axis=1).T.reshape(8, 32, rank)

    wait(wy_recv.at[0:ny * NC - 1], wy_rs)
    total = wy_recv[0]
    for i in range(1, ny * NC):
        total = total + wy_recv[i]
    if nx > 1:
        wx_send[...] = total
        start(nx, x, dev_x, lambda t: wx_send, wx_recv.at[x], wx_ss, wx_rs)
        wx_recv[x] = total
        wait(wx_recv.at[0:nx - 1], wx_rs)
        total = wx_recv[0]
        for i in range(1, nx):
            total = total + wx_recv[i]
    last = total[half:half + 8]
    g_rows = jnp.concatenate([total[0:half, pb:pb + 32],
                              jnp.concatenate([last[:, 16 * i:16 * i + 16] for i in range(3)], axis=0)], axis=1)
    denom_w = dot(g_rows, wm_send[0:rank, :])
    denom_w = jnp.where(lax.broadcasted_iota(jnp.int32, (half, 128), 1) < pb, denom_w, 1.0)
    w_new = wm_send[pl.ds(pl.multiple_of(c * half, 8), half), :] * total[0:half] / denom_w
    mine_w = pl.ds(pl.multiple_of(c * half, 8), half)
    wz_send[...] = w_new
    start(*peers_z, lambda t: wz_send, wz_recv.at[z, mine_w, :], wz_ss, wz_rs)
    wz_recv[z, mine_w, :] = w_new
    wait(wz_recv.at[0:nz - 1, 0:half, :], wz_rs)
    share = remote(wz_recv.at[:, mine_w, :], wz_recv.at[:, mine_w, :], wp_ss, wp_rs, partner)
    share.start()
    wait(rs_recv.at[3, 0:nz - 1], z_ss.at[3])
    wait(hz_recv.at[3, 0:nz - 1], g_ss.at[3])
    wait(hy_recv.at[3, 0:ny - 1], y_ss.at[3])
    wait(wy_recv.at[0:ny * NC - 1], wy_ss)
    if nx > 1:
        wait(wx_recv.at[0:nx - 1], wx_ss)
    wait(wz_recv.at[0:nz - 1, 0:half, :], wz_ss)
    share.wait()
    pieces = []
    for xd in range(nx):
        for zd in range(nz):
            pieces.append(wz_recv[zd][:, xd * zs:(xd + 1) * zs])
    w_out[...] = jnp.concatenate(pieces, axis=1)


def local(nx, ny, nz, cube, taps_x, taps_y, factor_w, factor_h):
    _, planes, sy, sx = cube.shape
    rank = factor_w.shape[2]
    w_t = factor_w[0].T
    h_t = factor_h.transpose(1, 2, 0)
    half = rank // 2
    nu = ny * nx * NC
    ks = nu * planes * (nz // 4)
    vmem = pl.BlockSpec(memory_space=pltpu.VMEM)
    anywhere = pl.BlockSpec(memory_space=pltpu.HBM)
    sem = pltpu.SemaphoreType.DMA

    def buf(*shape):
        return pltpu.VMEM(shape, F32)

    w_next, h_next = pl.pallas_call(
        functools.partial(kernel, (nx, ny, nz, planes)),
        out_shape=(buf(*w_t.shape), buf(*h_t.shape)),
        in_specs=[anywhere] * 5,
        out_specs=(vmem, vmem),
        scratch_shapes=[
            buf(planes, sy, sx), buf(planes, 1, taps_x.shape[2]), buf(planes, 1, taps_y.shape[2]), buf(*w_t.shape), buf(8, 32, rank),
            buf(8 * nu, ks // nu, 128), buf(8, ks, 128), buf(2 * rank, 128), buf(ny, 2 * rank, 128),
            buf(4, nz, half, 128), buf(4, nz, half, 128), buf(4, half, 128), buf(4, nz, half, 128), buf(4, ny, half, 128),
            buf(NC, ny, half + 8, 128), buf(ny * NC, half + 8, 128),
            buf(half + 8, 128), buf(nx, half + 8, 128), buf(half, 128), buf(nz, rank, 128),
            sem((planes,)), sem((4,)), sem((3, nu)), sem((3,)), sem, sem, sem((4,)), sem((4,)), sem((4,)), sem((4,)), sem((4,)), sem((4,)),
            sem, sem, sem, sem, sem, sem, sem, sem,
        ],
        compiler_params=pltpu.CompilerParams(collective_id=0, has_side_effects=True, vmem_limit_bytes=VL << 20),
        name="nmf",
    )(cube[0], taps_x.reshape(planes, 1, -1), taps_y.reshape(planes, 1, -1), w_t, h_t)
    return w_next.T[None], h_next.transpose(2, 0, 1)


def solution(mesh):
    n_sp, ny = mesh.shape["sp"], mesh.shape["bd"]
    nx, nz = (4, 8) if n_sp == 64 else (1, n_sp // NC)
    in_specs = (
        P("bd", "sp", None, None),
        P("bd", "sp", None),
        P("bd", "sp", None),
        P("bd", None, None),
        P(None, None, "sp"),
    )
    out_specs = (P("bd", None, None), P(None, None, "sp"))
    return jax.shard_map(functools.partial(local, nx, ny, nz), mesh=mesh, in_specs=in_specs, out_specs=out_specs, check_vma=False)
```

```python
import functools

import jax
import jax.numpy as jnp
from jax import lax
from jax.experimental import pallas as pl
from jax.experimental.pallas import tpu as pltpu
from jax.sharding import PartitionSpec as P

HI = lax.Precision.HIGHEST
MESH = pl.DeviceIdType.MESH
NC = 2
VL = 60
F32 = jnp.float32
ORDER = (0, 2, 1, 3)
ROWS = ((1,), (0,))
LANES = ((1,), (1,))


def dot(a, b, dims=ROWS):
    return lax.dot_general(a, b, (dims, ((), ())), precision=HI, preferred_element_type=F32)


def dot_t(a, b):
    return dot(a, b, LANES)


def split(a):
    high = a.astype(jnp.bfloat16)
    return high, (a - high.astype(F32)).astype(jnp.bfloat16)


def dot3(a, b, dims=ROWS):
    (ah, al), (bh, bl) = split(a), split(b)

    def one(p, q):
        return lax.dot_general(p, q, (dims, ((), ())), preferred_element_type=F32)

    return one(ah, bh) + (one(ah, bl) + one(al, bh))


def pad_lanes(a):
    if a.shape[1] == 128:
        return a
    return jnp.concatenate([a, jnp.zeros((a.shape[0], 128 - a.shape[1]), F32)], axis=1)


def kernel(geo, cube_hbm, tx_hbm, ty_hbm, w_hbm, h_hbm, w_out, h_out,
           cube, taps_x, taps_y, w_t, h_in, send, recv, wm_send, wm_recv, rs_send, rs_recv, hz_send, hz_recv, hy_recv,
           wc_send, wy_recv, wx_send, wx_recv, wz_send, wz_recv,
           cube_sem, in_sem, a_ss, a_rs, m_ss, m_rs, z_ss, z_rs, g_ss, g_rs, y_ss, y_rs,
           wy_ss, wy_rs, wx_ss, wx_rs, wz_ss, wz_rs, wp_ss, wp_rs):
    nx, ny, nz, planes = geo
    nh = nz // 4
    nxc = nx * NC
    nu = ny * nxc
    pb = nxc * planes
    ptot = ny * pb
    zs = NC * planes
    rpu = planes * nh
    ks = nu * rpu
    chunk = 8 // nh
    nj = planes // chunk
    rank = w_t.shape[0]
    half = rank // 2
    sy, sx = cube.shape[1], cube.shape[2]
    sp = lax.axis_index("sp")
    y = lax.axis_index("bd")
    c = lax.rem(sp, NC)
    z = lax.rem(sp // NC, nz)
    x = sp // (NC * nz)
    xc = x * NC + c
    u = y * nxc + xc

    def dev_z(t):
        return ((x * nz + t) * NC + c, y)

    def dev_y(t):
        return (sp, t)

    def dev_x(t):
        return ((t * nz + z) * NC + c, y)

    partner = (sp + 1 - 2 * c, y)

    barrier = pltpu.get_barrier_semaphore()

    def offsets():
        rounds = ((1, 1), (3, 3), (0, 2), (2, 0), (1, 3), (3, 1), (2, 2), (1, 2), (3, 0), (0, 1), (2, 3), (1, 0), (3, 2), (0, 3), (2, 1))
        steps = [d for d in rounds if d[0] < nx and d[1] < ny]
        return [(dx, dy, dc) for dc in range(NC) for dx, dy in steps] + [(0, 0, 1)]

    for dx, dy, dc in offsets():
        there = ((lax.rem(x + dx, nx) * nz + z) * NC + lax.rem(c + dc, NC), lax.rem(y + dy, ny))
        pl.semaphore_signal(barrier, inc=1, device_id=there, device_id_type=MESH)
    for dz in range(1, nz):
        pl.semaphore_signal(barrier, inc=1, device_id=dev_z(lax.rem(z + dz, nz)), device_id_type=MESH)

    tx_copy = pltpu.make_async_copy(tx_hbm, taps_x, in_sem.at[2])
    tx_copy.start()
    ty_copy = pltpu.make_async_copy(ty_hbm, taps_y, in_sem.at[3])
    ty_copy.start()
    for p in range(planes):
        pltpu.make_async_copy(cube_hbm.at[p], cube.at[p], cube_sem.at[p]).start()
    w_copy = pltpu.make_async_copy(w_hbm, w_t, in_sem.at[0])
    w_copy.start()
    h_copy = pltpu.make_async_copy(h_hbm.at[pl.ds(y * 8, 8)], h_in, in_sem.at[1])
    h_copy.start()

    def remote(src, dst, ss, rs, dev):
        return pltpu.make_async_remote_copy(src_ref=src, dst_ref=dst, send_sem=ss, recv_sem=rs, device_id=dev, device_id_type=MESH)

    def start(n, me, dev, src, dst, ss, rs):
        @pl.loop(1, n)
        def _(k):
            t = lax.rem(me + k, n)
            remote(src(t), dst, ss, rs, dev(t)).start()

    def wait(ref, sem):
        pltpu.make_async_copy(ref, ref, sem).wait()

    lane = lax.broadcasted_iota(jnp.int32, (8, 128), 1)
    even = ((lane >= 0) & (lane < 32)) | ((lane >= 64) & (lane < 96))
    nb = sx // 128
    vx = nb // nx
    lane_l = lax.broadcasted_iota(jnp.int32, (sy * nb, 128), 1)
    from_left = lane_l >= 116
    from_right = lane_l < 12
    band_o = lax.broadcasted_iota(jnp.int32, (128, 128), 0)
    band_i = lax.broadcasted_iota(jnp.int32, (128, 128), 1)
    centre = (band_i - band_o < 64) & (band_o - band_i < 64)
    send_flat = send.reshape(8 * ks, 128)

    def band(taps, size):
        t = taps / jnp.sum(taps, axis=1, keepdims=True)
        t = pltpu.roll(jnp.broadcast_to(pad_lanes(t), (size, 128)), 116, 1)
        return pltpu.roll(t, 0, 1, stride=1, stride_axis=0)

    def blur(p):
        rows = dot3(band(taps_y[p], sy)[:, 0:sy], cube[p])
        own = jnp.concatenate([rows[:, 128 * b:128 * b + 128] for b in range(nb)], axis=0)
        zero = jnp.zeros((sy, 128), F32)
        left = jnp.concatenate([zero, own[:-sy]], axis=0)
        right = jnp.concatenate([own[sy:], zero], axis=0)
        edge = jnp.where(from_left, left, jnp.where(from_right, right, 0.0))
        table = band(taps_x[p], 128)
        table = jnp.concatenate([jnp.where(centre, table, 0.0), jnp.where(centre, 0.0, table)], axis=1)
        out = dot3(jnp.concatenate([own, edge], axis=1), table, LANES)
        for q in range(ny):
            for xd in range(nx):
                for h in range(nh):
                    b0 = xd * vx + 2 * h
                    a0 = out[b0 * sy + q * 8:b0 * sy + q * 8 + 8]
                    a1 = out[(b0 + 1) * sy + q * 8:(b0 + 1) * sy + q * 8 + 8]
                    v0 = jnp.where(even, a0, pltpu.roll(a1, 32, 1))
                    v1 = jnp.where(even, pltpu.roll(a0, 96, 1), a1)
                    for cd, v in ((0, v0), (1, v1)):
                        d = (q * nx + xd) * NC + cd
                        send_flat[pl.ds(d * 8 * rpu + p * nh + h, 8, stride=rpu), :] = v

    def a2a(k0, nk, row, rows, sem, after=None):
        for i, (dx, dy, dc) in enumerate(offsets()):
            tx, ty, tc = lax.rem(x + dx, nx), lax.rem(y + dy, ny), lax.rem(c + dc, NC)
            t = (ty * nx + tx) * NC + tc
            if after is not None:
                wait(recv.at[0:after, 0:rpu, :], a_ss.at[sem - 1, i])
            remote(send.at[pl.ds(t * 8 + k0, nk), pl.ds(row, rows), :],
                   recv.at[pl.ds(k0, nk), pl.ds(pl.multiple_of(u * rpu + row, 8), rows), :],
                   a_ss.at[sem, i], a_rs.at[sem], ((tx * nz + z) * NC + tc, ty)).start()

    tx_copy.wait()
    ty_copy.wait()

    @pl.loop(0, nj)
    def _(j):
        for i in range(chunk):
            p = j * chunk + i
            pltpu.make_async_copy(cube_hbm.at[p], cube.at[p], cube_sem.at[p]).wait()
        for i in range(chunk):
            blur(j * chunk + i)

        @pl.when(j == 0)
        def _():
            w_copy.wait()
            l_i = lax.broadcasted_iota(jnp.int32, (w_t.shape[1], 128), 0)
            j_i = lax.broadcasted_iota(jnp.int32, (w_t.shape[1], 128), 1)
            xj = jnp.zeros_like(j_i)
            for i in range(1, nx):
                xj = xj + jnp.where(j_i >= zs * i, 1, 0)
            target = xj * (nz * zs) + z * zs + (j_i - zs * xj)
            pick = jnp.where((l_i == target) & (j_i < pb), 1.0, 0.0).astype(F32)
            w_all = w_t[...]
            w_slice = dot(w_all, pick)
            wm_send[0:rank, :] = w_slice
            wm_send[rank:2 * rank, :] = pad_lanes(dot_t(w_all, w_all))
            wm_recv[y] = wm_send[...]
            pl.semaphore_wait(barrier, nu + nz - 2)
            start(ny, y, dev_y, lambda t: wm_send, wm_recv.at[y], m_ss, m_rs)

        a2a(0, 4, pl.multiple_of(j * 8, 8), 8, 0)

    mine = pl.ds(pl.multiple_of(u * rpu, 8), rpu)
    for k in range(8):
        recv[k, mine, :] = send[u * 8 + k]

    def packed(a, q):
        return jnp.concatenate([a[0:half, 64 * q:64 * q + 64], a[half:rank, 64 * q:64 * q + 64]], axis=1)

    def regroup(blocks, g):
        lane_r = lax.broadcasted_iota(jnp.int32, (half, 128), 1)
        out = None
        for i, blk in enumerate(blocks):
            moved = blk if i == g else pltpu.roll(blk, (32 * (i - g)) % 128, 1)
            out = moved if out is None else jnp.where(lane_r >= 32 * i, moved, out)
        return out

    def x_of(s):
        return jnp.concatenate([recv[s, pl.ds(h, ptot, stride=nh), :] for h in range(nh)], axis=1)

    peers_z = (nz, z, dev_z)

    def contract(q):
        parts = [dot(w_z, x_of(2 * q + i)) for i in range(2)]
        for h in range(nh):
            cols = [p[:, 128 * h:128 * h + 128] for p in parts]
            blocks = [cols[0][0:half], cols[1][0:half], cols[0][half:rank], cols[1][half:rank]]
            for g in range(4):
                rs_send[q, 4 * h + ORDER[g]] = regroup(blocks, g)
        start(*peers_z, lambda t: rs_send.at[q, t], rs_recv.at[q, z], z_ss.at[q], z_rs.at[q])
        rs_recv[q, z] = rs_send[q, z]

    def update(q):
        wait(rs_recv.at[q, 0:nz - 1], z_rs.at[q])
        numer = rs_recv[q, 0]
        for i in range(1, nz):
            numer = numer + rs_recv[q, i]
        h_next = packed(h_own, q) * numer / packed(denom, q)
        hz_send[q] = h_next
        start(*peers_z, lambda t: hz_send.at[q], hz_recv.at[q, z], g_ss.at[q], g_rs.at[q])
        start(ny, y, dev_y, lambda t: hz_send.at[q], hy_recv.at[q, y], y_ss.at[q], y_rs.at[q])
        hz_recv[q, z] = h_next
        hy_recv[q, y] = h_next

    def gather(q, sums):
        wait(hz_recv.at[q, 0:nz - 1], g_rs.at[q])
        for i in range(2):
            cols = []
            for h in range(nh):
                blocks = [hz_recv[q, 4 * h + ORDER[g]] for g in range(4)]
                cols.append(jnp.concatenate([regroup(blocks, i), regroup(blocks, 2 + i)], axis=0))
            h_s = jnp.concatenate(cols, axis=1)
            new = (dot_t(x_of(2 * q + i), h_s), dot_t(h_s, h_s))
            sums = new if sums is None else (sums[0] + new[0], sums[1] + new[1])
        return sums

    first_half = recv.at[0:4, 0:(nu - 1) * rpu, :]
    quarter = recv.at[0:2, 0:(nu - 1) * rpu, :]
    a2a(4, 2, 0, rpu, 1, after=4)
    wait(wm_recv.at[0:ny - 1], m_rs)
    w_z = jnp.concatenate([wm_recv[b][0:rank, 0:pb] for b in range(ny)], axis=1)
    gram_w = sum(wm_recv[b][rank:2 * rank, 0:rank] for b in range(ny))
    h_copy.wait()
    h_own = h_in[...].reshape(256, rank).T
    denom = dot(gram_w, h_own)
    wait(first_half, a_rs.at[0])
    contract(0)
    contract(1)
    a2a(6, 2, 0, rpu, 2, after=2)
    wait(quarter, a_rs.at[1])
    contract(2)
    update(0)
    update(1)
    wait(quarter, a_rs.at[2])
    contract(3)
    update(2)
    sums = gather(0, None)
    sums = gather(1, sums)
    for i in range(nu - 1):
        wait(recv.at[0:2, 0:rpu, :], a_ss.at[2, i])
    update(3)
    sums = gather(2, sums)
    for q in range(3):
        wait(rs_recv.at[q, 0:nz - 1], z_ss.at[q])
        wait(hz_recv.at[q, 0:nz - 1], g_ss.at[q])
        wait(hy_recv.at[q, 0:ny - 1], y_ss.at[q])
    wait(wm_recv.at[0:ny - 1], m_ss)
    sums = gather(3, sums)
    numer_w, gram_h = sums

    for f in range(2):
        g_half = gram_h[f * half:(f + 1) * half]
        tail = pad_lanes(jnp.concatenate([g_half[8 * i:8 * i + 8, 32:48] for i in range(3)], axis=1))
        for b in range(ny):
            num = numer_w[b * pb:(b + 1) * pb].T[f * half:(f + 1) * half]
            wc_send[f, b, 0:half, :] = pad_lanes(jnp.concatenate([num, g_half[:, 0:32]], axis=1))
            wc_send[f, b, half:half + 8, :] = tail
    for dc in range(NC):
        tc = lax.rem(c + dc, NC)
        for dy in range(ny):
            ty = lax.rem(y + dy, ny)
            if dy or dc:
                remote(wc_send.at[tc, ty], wy_recv.at[y * NC + c], wy_ss, wy_rs, (sp - c + tc, ty)).start()
    wy_recv[y * NC + c] = wc_send[c, y]

    for q in range(4):
        wait(hy_recv.at[q, 0:ny - 1], y_rs.at[q])
    for b in range(ny):
        cols = []
        for q in range(4):
            v = hy_recv[q, b]
            cols.append(jnp.concatenate([v[:, 0:64], v[:, 64:128]], axis=0))
        h_out[8 * b:8 * b + 8] = jnp.concatenate(cols, axis=1).T.reshape(8, 32, rank)

    wait(wy_recv.at[0:ny * NC - 1], wy_rs)
    total = wy_recv[0]
    for i in range(1, ny * NC):
        total = total + wy_recv[i]
    if nx > 1:
        wx_send[...] = total
        start(nx, x, dev_x, lambda t: wx_send, wx_recv.at[x], wx_ss, wx_rs)
        wx_recv[x] = total
        wait(wx_recv.at[0:nx - 1], wx_rs)
        total = wx_recv[0]
        for i in range(1, nx):
            total = total + wx_recv[i]
    last = total[half:half + 8]
    g_rows = jnp.concatenate([total[0:half, pb:pb + 32],
                              jnp.concatenate([last[:, 16 * i:16 * i + 16] for i in range(3)], axis=0)], axis=1)
    denom_w = dot(g_rows, wm_send[0:rank, :])
    denom_w = jnp.where(lax.broadcasted_iota(jnp.int32, (half, 128), 1) < pb, denom_w, 1.0)
    w_new = wm_send[pl.ds(pl.multiple_of(c * half, 8), half), :] * total[0:half] / denom_w
    mine_w = pl.ds(pl.multiple_of(c * half, 8), half)
    wz_send[...] = w_new
    start(*peers_z, lambda t: wz_send, wz_recv.at[z, mine_w, :], wz_ss, wz_rs)
    wz_recv[z, mine_w, :] = w_new
    wait(wz_recv.at[0:nz - 1, 0:half, :], wz_rs)
    share = remote(wz_recv.at[:, mine_w, :], wz_recv.at[:, mine_w, :], wp_ss, wp_rs, partner)
    share.start()
    wait(rs_recv.at[3, 0:nz - 1], z_ss.at[3])
    wait(hz_recv.at[3, 0:nz - 1], g_ss.at[3])
    wait(hy_recv.at[3, 0:ny - 1], y_ss.at[3])
    wait(wy_recv.at[0:ny * NC - 1], wy_ss)
    if nx > 1:
        wait(wx_recv.at[0:nx - 1], wx_ss)
    wait(wz_recv.at[0:nz - 1, 0:half, :], wz_ss)
    share.wait()
    pieces = []
    for xd in range(nx):
        for zd in range(nz):
            pieces.append(wz_recv[zd][:, xd * zs:(xd + 1) * zs])
    w_out[...] = jnp.concatenate(pieces, axis=1)


def local(nx, ny, nz, cube, taps_x, taps_y, factor_w, factor_h):
    _, planes, sy, sx = cube.shape
    rank = factor_w.shape[2]
    w_t = factor_w[0].T
    h_t = factor_h.transpose(1, 2, 0)
    half = rank // 2
    nu = ny * nx * NC
    ks = nu * planes * (nz // 4)
    vmem = pl.BlockSpec(memory_space=pltpu.VMEM)
    anywhere = pl.BlockSpec(memory_space=pltpu.HBM)
    sem = pltpu.SemaphoreType.DMA

    def buf(*shape):
        return pltpu.VMEM(shape, F32)

    w_next, h_next = pl.pallas_call(
        functools.partial(kernel, (nx, ny, nz, planes)),
        out_shape=(buf(*w_t.shape), buf(*h_t.shape)),
        in_specs=[anywhere] * 5,
        out_specs=(vmem, vmem),
        scratch_shapes=[
            buf(planes, sy, sx), buf(planes, 1, taps_x.shape[2]), buf(planes, 1, taps_y.shape[2]), buf(*w_t.shape), buf(8, 32, rank),
            buf(8 * nu, ks // nu, 128), buf(8, ks, 128), buf(2 * rank, 128), buf(ny, 2 * rank, 128),
            buf(4, nz, half, 128), buf(4, nz, half, 128), buf(4, half, 128), buf(4, nz, half, 128), buf(4, ny, half, 128),
            buf(NC, ny, half + 8, 128), buf(ny * NC, half + 8, 128),
            buf(half + 8, 128), buf(nx, half + 8, 128), buf(half, 128), buf(nz, rank, 128),
            sem((planes,)), sem((4,)), sem((3, nu)), sem((3,)), sem, sem, sem((4,)), sem((4,)), sem((4,)), sem((4,)), sem((4,)), sem((4,)),
            sem, sem, sem, sem, sem, sem, sem, sem,
        ],
        compiler_params=pltpu.CompilerParams(collective_id=0, has_side_effects=True, vmem_limit_bytes=VL << 20),
        name="nmf",
    )(cube[0], taps_x.reshape(planes, 1, -1), taps_y.reshape(planes, 1, -1), w_t, h_t)
    return w_next.T[None], h_next.transpose(2, 0, 1)


def solution(mesh):
    n_sp, ny = mesh.shape["sp"], mesh.shape["bd"]
    nx, nz = (4, 8) if n_sp == 64 else (1, n_sp // NC)
    in_specs = (
        P("bd", "sp", None, None),
        P("bd", "sp", None),
        P("bd", "sp", None),
        P("bd", None, None),
        P(None, None, "sp"),
    )
    out_specs = (P("bd", None, None), P(None, None, "sp"))
    return jax.shard_map(functools.partial(local, nx, ny, nz), mesh=mesh, in_specs=in_specs, out_specs=out_specs, check_vma=False)
```

```python
import functools

import jax
import jax.numpy as jnp
from jax import lax
from jax.experimental import pallas as pl
from jax.experimental.pallas import tpu as pltpu
from jax.sharding import PartitionSpec as P

HI = lax.Precision.HIGHEST
MESH = pl.DeviceIdType.MESH
NC = 2
VL = 60
F32 = jnp.float32
ORDER = (0, 2, 1, 3)
ROWS = ((1,), (0,))
LANES = ((1,), (1,))


def dot(a, b, dims=ROWS):
    return lax.dot_general(a, b, (dims, ((), ())), precision=HI, preferred_element_type=F32)


def dot_t(a, b):
    return dot(a, b, LANES)


def split(a):
    high = a.astype(jnp.bfloat16)
    return high, (a - high.astype(F32)).astype(jnp.bfloat16)


def dot3(a, b, dims=ROWS):
    (ah, al), (bh, bl) = split(a), split(b)

    def one(p, q):
        return lax.dot_general(p, q, (dims, ((), ())), preferred_element_type=F32)

    return one(ah, bh) + (one(ah, bl) + one(al, bh))


def pad_lanes(a):
    if a.shape[1] == 128:
        return a
    return jnp.concatenate([a, jnp.zeros((a.shape[0], 128 - a.shape[1]), F32)], axis=1)


def kernel(geo, cube_hbm, tx_hbm, ty_hbm, w_hbm, h_hbm, w_out, h_out,
           cube, taps_x, taps_y, w_t, h_in, send, recv, wm_send, wm_recv, rs_send, rs_recv, hz_send, hz_recv, hy_recv,
           wc_send, wy_recv, wx_send, wx_recv, wz_send, wz_recv,
           cube_sem, in_sem, a_ss, a_rs, m_ss, m_rs, z_ss, z_rs, g_ss, g_rs, y_ss, y_rs,
           wy_ss, wy_rs, wx_ss, wx_rs, wz_ss, wz_rs, wp_ss, wp_rs):
    nx, ny, nz, planes = geo
    nh = nz // 4
    nxc = nx * NC
    nu = ny * nxc
    pb = nxc * planes
    ptot = ny * pb
    zs = NC * planes
    rpu = planes * nh
    ks = nu * rpu
    chunk = 8 // nh
    nj = planes // chunk
    rank = w_t.shape[0]
    half = rank // 2
    sy, sx = cube.shape[1], cube.shape[2]
    sp = lax.axis_index("sp")
    y = lax.axis_index("bd")
    c = lax.rem(sp, NC)
    z = lax.rem(sp // NC, nz)
    x = sp // (NC * nz)
    xc = x * NC + c
    u = y * nxc + xc

    def dev_z(t):
        return ((x * nz + t) * NC + c, y)

    def dev_y(t):
        return (sp, t)

    def dev_x(t):
        return ((t * nz + z) * NC + c, y)

    partner = (sp + 1 - 2 * c, y)

    barrier = pltpu.get_barrier_semaphore()

    def offsets():
        rounds = ((1, 1), (3, 3), (0, 2), (2, 0), (1, 3), (3, 1), (2, 2), (1, 2), (3, 0), (0, 1), (2, 3), (1, 0), (3, 2), (0, 3), (2, 1))
        steps = [d for d in rounds if d[0] < nx and d[1] < ny]
        return [(dx, dy, dc) for dc in range(NC) for dx, dy in steps] + [(0, 0, 1)]

    for dx, dy, dc in offsets():
        there = ((lax.rem(x + dx, nx) * nz + z) * NC + lax.rem(c + dc, NC), lax.rem(y + dy, ny))
        pl.semaphore_signal(barrier, inc=1, device_id=there, device_id_type=MESH)
    for dz in range(1, nz):
        pl.semaphore_signal(barrier, inc=1, device_id=dev_z(lax.rem(z + dz, nz)), device_id_type=MESH)

    tx_copy = pltpu.make_async_copy(tx_hbm, taps_x, in_sem.at[2])
    tx_copy.start()
    ty_copy = pltpu.make_async_copy(ty_hbm, taps_y, in_sem.at[3])
    ty_copy.start()
    for p in range(planes):
        pltpu.make_async_copy(cube_hbm.at[p], cube.at[p], cube_sem.at[p]).start()
    w_copy = pltpu.make_async_copy(w_hbm, w_t, in_sem.at[0])
    w_copy.start()
    h_copy = pltpu.make_async_copy(h_hbm.at[pl.ds(y * 8, 8)], h_in, in_sem.at[1])
    h_copy.start()

    def remote(src, dst, ss, rs, dev):
        return pltpu.make_async_remote_copy(src_ref=src, dst_ref=dst, send_sem=ss, recv_sem=rs, device_id=dev, device_id_type=MESH)

    def start(n, me, dev, src, dst, ss, rs):
        @pl.loop(1, n)
        def _(k):
            t = lax.rem(me + k, n)
            remote(src(t), dst, ss, rs, dev(t)).start()

    def wait(ref, sem):
        pltpu.make_async_copy(ref, ref, sem).wait()

    lane = lax.broadcasted_iota(jnp.int32, (8, 128), 1)
    even = ((lane >= 0) & (lane < 32)) | ((lane >= 64) & (lane < 96))
    nb = sx // 128
    vx = nb // nx
    lane_l = lax.broadcasted_iota(jnp.int32, (sy * nb, 128), 1)
    from_left = lane_l >= 116
    from_right = lane_l < 12
    band_o = lax.broadcasted_iota(jnp.int32, (128, 128), 0)
    band_i = lax.broadcasted_iota(jnp.int32, (128, 128), 1)
    centre = (band_i - band_o < 64) & (band_o - band_i < 64)
    send_flat = send.reshape(8 * ks, 128)

    def band(taps, size):
        t = taps / jnp.sum(taps, axis=1, keepdims=True)
        t = pltpu.roll(jnp.broadcast_to(pad_lanes(t), (size, 128)), 116, 1)
        return pltpu.roll(t, 0, 1, stride=1, stride_axis=0)

    def blur(p):
        rows = dot3(band(taps_y[p], sy)[:, 0:sy], cube[p])
        own = jnp.concatenate([rows[:, 128 * b:128 * b + 128] for b in range(nb)], axis=0)
        zero = jnp.zeros((sy, 128), F32)
        left = jnp.concatenate([zero, own[:-sy]], axis=0)
        right = jnp.concatenate([own[sy:], zero], axis=0)
        edge = jnp.where(from_left, left, jnp.where(from_right, right, 0.0))
        table = band(taps_x[p], 128)
        table = jnp.concatenate([jnp.where(centre, table, 0.0), jnp.where(centre, 0.0, table)], axis=1)
        out = dot3(jnp.concatenate([own, edge], axis=1), table, LANES)
        for q in range(ny):
            for xd in range(nx):
                for h in range(nh):
                    b0 = xd * vx + 2 * h
                    a0 = out[b0 * sy + q * 8:b0 * sy + q * 8 + 8]
                    a1 = out[(b0 + 1) * sy + q * 8:(b0 + 1) * sy + q * 8 + 8]
                    v0 = jnp.where(even, a0, pltpu.roll(a1, 32, 1))
                    v1 = jnp.where(even, pltpu.roll(a0, 96, 1), a1)
                    for cd, v in ((0, v0), (1, v1)):
                        d = (q * nx + xd) * NC + cd
                        send_flat[pl.ds(d * 8 * rpu + p * nh + h, 8, stride=rpu), :] = v

    def a2a(k0, nk, row, rows, sem, after=None):
        for i, (dx, dy, dc) in enumerate(offsets()):
            tx, ty, tc = lax.rem(x + dx, nx), lax.rem(y + dy, ny), lax.rem(c + dc, NC)
            t = (ty * nx + tx) * NC + tc
            if after is not None:
                wait(recv.at[0:after, 0:rpu, :], a_ss.at[sem - 1, i])
            remote(send.at[pl.ds(t * 8 + k0, nk), pl.ds(row, rows), :],
                   recv.at[pl.ds(k0, nk), pl.ds(pl.multiple_of(u * rpu + row, 8), rows), :],
                   a_ss.at[sem, i], a_rs.at[sem], ((tx * nz + z) * NC + tc, ty)).start()

    tx_copy.wait()
    ty_copy.wait()

    @pl.loop(0, nj)
    def _(j):
        for i in range(chunk):
            p = j * chunk + i
            pltpu.make_async_copy(cube_hbm.at[p], cube.at[p], cube_sem.at[p]).wait()
        for i in range(chunk):
            blur(j * chunk + i)

        @pl.when(j == 0)
        def _():
            w_copy.wait()
            l_i = lax.broadcasted_iota(jnp.int32, (w_t.shape[1], 128), 0)
            j_i = lax.broadcasted_iota(jnp.int32, (w_t.shape[1], 128), 1)
            xj = jnp.zeros_like(j_i)
            for i in range(1, nx):
                xj = xj + jnp.where(j_i >= zs * i, 1, 0)
            target = xj * (nz * zs) + z * zs + (j_i - zs * xj)
            pick = jnp.where((l_i == target) & (j_i < pb), 1.0, 0.0).astype(F32)
            w_all = w_t[...]
            w_slice = dot(w_all, pick)
            wm_send[0:rank, :] = w_slice
            wm_send[rank:2 * rank, :] = pad_lanes(dot_t(w_all, w_all))
            wm_recv[y] = wm_send[...]
            pl.semaphore_wait(barrier, nu + nz - 2)
            start(ny, y, dev_y, lambda t: wm_send, wm_recv.at[y], m_ss, m_rs)

        a2a(0, 4, pl.multiple_of(j * 8, 8), 8, 0)

    mine = pl.ds(pl.multiple_of(u * rpu, 8), rpu)
    for k in range(8):
        recv[k, mine, :] = send[u * 8 + k]

    def packed(a, q):
        return jnp.concatenate([a[0:half, 64 * q:64 * q + 64], a[half:rank, 64 * q:64 * q + 64]], axis=1)

    def regroup(blocks, g):
        lane_r = lax.broadcasted_iota(jnp.int32, (half, 128), 1)
        out = None
        for i, blk in enumerate(blocks):
            moved = blk if i == g else pltpu.roll(blk, (32 * (i - g)) % 128, 1)
            out = moved if out is None else jnp.where(lane_r >= 32 * i, moved, out)
        return out

    def x_of(s):
        return jnp.concatenate([recv[s, pl.ds(h, ptot, stride=nh), :] for h in range(nh)], axis=1)

    peers_z = (nz, z, dev_z)

    def contract(q):
        parts = [dot3(w_z, x_of(2 * q + i)) for i in range(2)]
        for h in range(nh):
            cols = [p[:, 128 * h:128 * h + 128] for p in parts]
            blocks = [cols[0][0:half], cols[1][0:half], cols[0][half:rank], cols[1][half:rank]]
            for g in range(4):
                rs_send[q, 4 * h + ORDER[g]] = regroup(blocks, g)
        start(*peers_z, lambda t: rs_send.at[q, t], rs_recv.at[q, z], z_ss.at[q], z_rs.at[q])
        rs_recv[q, z] = rs_send[q, z]

    def update(q):
        wait(rs_recv.at[q, 0:nz - 1], z_rs.at[q])
        numer = rs_recv[q, 0]
        for i in range(1, nz):
            numer = numer + rs_recv[q, i]
        h_next = packed(h_own, q) * numer / packed(denom, q)
        hz_send[q] = h_next
        start(*peers_z, lambda t: hz_send.at[q], hz_recv.at[q, z], g_ss.at[q], g_rs.at[q])
        start(ny, y, dev_y, lambda t: hz_send.at[q], hy_recv.at[q, y], y_ss.at[q], y_rs.at[q])
        hz_recv[q, z] = h_next
        hy_recv[q, y] = h_next

    def gather(q, sums):
        wait(hz_recv.at[q, 0:nz - 1], g_rs.at[q])
        for i in range(2):
            cols = []
            for h in range(nh):
                blocks = [hz_recv[q, 4 * h + ORDER[g]] for g in range(4)]
                cols.append(jnp.concatenate([regroup(blocks, i), regroup(blocks, 2 + i)], axis=0))
            h_s = jnp.concatenate(cols, axis=1)
            new = (dot3(x_of(2 * q + i), h_s, LANES), dot_t(h_s, h_s))
            sums = new if sums is None else (sums[0] + new[0], sums[1] + new[1])
        return sums

    first_half = recv.at[0:4, 0:(nu - 1) * rpu, :]
    quarter = recv.at[0:2, 0:(nu - 1) * rpu, :]
    a2a(4, 2, 0, rpu, 1, after=4)
    wait(wm_recv.at[0:ny - 1], m_rs)
    w_z = jnp.concatenate([wm_recv[b][0:rank, 0:pb] for b in range(ny)], axis=1)
    gram_w = sum(wm_recv[b][rank:2 * rank, 0:rank] for b in range(ny))
    h_copy.wait()
    h_own = h_in[...].reshape(256, rank).T
    denom = dot(gram_w, h_own)
    wait(first_half, a_rs.at[0])
    contract(0)
    contract(1)
    a2a(6, 2, 0, rpu, 2, after=2)
    wait(quarter, a_rs.at[1])
    contract(2)
    update(0)
    update(1)
    wait(quarter, a_rs.at[2])
    contract(3)
    update(2)
    sums = gather(0, None)
    sums = gather(1, sums)
    for i in range(nu - 1):
        wait(recv.at[0:2, 0:rpu, :], a_ss.at[2, i])
    update(3)
    sums = gather(2, sums)
    for q in range(3):
        wait(rs_recv.at[q, 0:nz - 1], z_ss.at[q])
        wait(hz_recv.at[q, 0:nz - 1], g_ss.at[q])
        wait(hy_recv.at[q, 0:ny - 1], y_ss.at[q])
    wait(wm_recv.at[0:ny - 1], m_ss)
    sums = gather(3, sums)
    numer_w, gram_h = sums

    for f in range(2):
        g_half = gram_h[f * half:(f + 1) * half]
        tail = pad_lanes(jnp.concatenate([g_half[8 * i:8 * i + 8, 32:48] for i in range(3)], axis=1))
        for b in range(ny):
            num = numer_w[b * pb:(b + 1) * pb].T[f * half:(f + 1) * half]
            wc_send[f, b, 0:half, :] = pad_lanes(jnp.concatenate([num, g_half[:, 0:32]], axis=1))
            wc_send[f, b, half:half + 8, :] = tail
    for dc in range(NC):
        tc = lax.rem(c + dc, NC)
        for dy in range(ny):
            ty = lax.rem(y + dy, ny)
            if dy or dc:
                remote(wc_send.at[tc, ty], wy_recv.at[y * NC + c], wy_ss, wy_rs, (sp - c + tc, ty)).start()
    wy_recv[y * NC + c] = wc_send[c, y]

    for q in range(4):
        wait(hy_recv.at[q, 0:ny - 1], y_rs.at[q])
    for b in range(ny):
        cols = []
        for q in range(4):
            v = hy_recv[q, b]
            cols.append(jnp.concatenate([v[:, 0:64], v[:, 64:128]], axis=0))
        h_out[8 * b:8 * b + 8] = jnp.concatenate(cols, axis=1).T.reshape(8, 32, rank)

    wait(wy_recv.at[0:ny * NC - 1], wy_rs)
    total = wy_recv[0]
    for i in range(1, ny * NC):
        total = total + wy_recv[i]
    if nx > 1:
        wx_send[...] = total
        start(nx, x, dev_x, lambda t: wx_send, wx_recv.at[x], wx_ss, wx_rs)
        wx_recv[x] = total
        wait(wx_recv.at[0:nx - 1], wx_rs)
        total = wx_recv[0]
        for i in range(1, nx):
            total = total + wx_recv[i]
    last = total[half:half + 8]
    g_rows = jnp.concatenate([total[0:half, pb:pb + 32],
                              jnp.concatenate([last[:, 16 * i:16 * i + 16] for i in range(3)], axis=0)], axis=1)
    denom_w = dot(g_rows, wm_send[0:rank, :])
    denom_w = jnp.where(lax.broadcasted_iota(jnp.int32, (half, 128), 1) < pb, denom_w, 1.0)
    w_new = wm_send[pl.ds(pl.multiple_of(c * half, 8), half), :] * total[0:half] / denom_w
    mine_w = pl.ds(pl.multiple_of(c * half, 8), half)
    wz_send[...] = w_new
    start(*peers_z, lambda t: wz_send, wz_recv.at[z, mine_w, :], wz_ss, wz_rs)
    wz_recv[z, mine_w, :] = w_new
    wait(wz_recv.at[0:nz - 1, 0:half, :], wz_rs)
    share = remote(wz_recv.at[:, mine_w, :], wz_recv.at[:, mine_w, :], wp_ss, wp_rs, partner)
    share.start()
    wait(rs_recv.at[3, 0:nz - 1], z_ss.at[3])
    wait(hz_recv.at[3, 0:nz - 1], g_ss.at[3])
    wait(hy_recv.at[3, 0:ny - 1], y_ss.at[3])
    wait(wy_recv.at[0:ny * NC - 1], wy_ss)
    if nx > 1:
        wait(wx_recv.at[0:nx - 1], wx_ss)
    wait(wz_recv.at[0:nz - 1, 0:half, :], wz_ss)
    share.wait()
    pieces = []
    for xd in range(nx):
        for zd in range(nz):
            pieces.append(wz_recv[zd][:, xd * zs:(xd + 1) * zs])
    w_out[...] = jnp.concatenate(pieces, axis=1)


def local(nx, ny, nz, cube, taps_x, taps_y, factor_w, factor_h):
    _, planes, sy, sx = cube.shape
    rank = factor_w.shape[2]
    w_t = factor_w[0].T
    h_t = factor_h.transpose(1, 2, 0)
    half = rank // 2
    nu = ny * nx * NC
    ks = nu * planes * (nz // 4)
    vmem = pl.BlockSpec(memory_space=pltpu.VMEM)
    anywhere = pl.BlockSpec(memory_space=pltpu.HBM)
    sem = pltpu.SemaphoreType.DMA

    def buf(*shape):
        return pltpu.VMEM(shape, F32)

    w_next, h_next = pl.pallas_call(
        functools.partial(kernel, (nx, ny, nz, planes)),
        out_shape=(buf(*w_t.shape), buf(*h_t.shape)),
        in_specs=[anywhere] * 5,
        out_specs=(vmem, vmem),
        scratch_shapes=[
            buf(planes, sy, sx), buf(planes, 1, taps_x.shape[2]), buf(planes, 1, taps_y.shape[2]), buf(*w_t.shape), buf(8, 32, rank),
            buf(8 * nu, ks // nu, 128), buf(8, ks, 128), buf(2 * rank, 128), buf(ny, 2 * rank, 128),
            buf(4, nz, half, 128), buf(4, nz, half, 128), buf(4, half, 128), buf(4, nz, half, 128), buf(4, ny, half, 128),
            buf(NC, ny, half + 8, 128), buf(ny * NC, half + 8, 128),
            buf(half + 8, 128), buf(nx, half + 8, 128), buf(half, 128), buf(nz, rank, 128),
            sem((planes,)), sem((4,)), sem((3, nu)), sem((3,)), sem, sem, sem((4,)), sem((4,)), sem((4,)), sem((4,)), sem((4,)), sem((4,)),
            sem, sem, sem, sem, sem, sem, sem, sem,
        ],
        compiler_params=pltpu.CompilerParams(collective_id=0, has_side_effects=True, vmem_limit_bytes=VL << 20),
        name="nmf",
    )(cube[0], taps_x.reshape(planes, 1, -1), taps_y.reshape(planes, 1, -1), w_t, h_t)
    return w_next.T[None], h_next.transpose(2, 0, 1)


def solution(mesh):
    n_sp, ny = mesh.shape["sp"], mesh.shape["bd"]
    nx, nz = (4, 8) if n_sp == 64 else (1, n_sp // NC)
    in_specs = (
        P("bd", "sp", None, None),
        P("bd", "sp", None),
        P("bd", "sp", None),
        P("bd", None, None),
        P(None, None, "sp"),
    )
    out_specs = (P("bd", None, None), P(None, None, "sp"))
    return jax.shard_map(functools.partial(local, nx, ny, nz), mesh=mesh, in_specs=in_specs, out_specs=out_specs, check_vma=False)
```
